256 devices in a mesh: seq: 16 (over y_lo, z), head: 16 (over y_hi, x, core).
Axes of the slice: x: 4, y: 4 (y_hi: 2, y_lo: 2; y = y_hi * 2 + y_lo), z: 8, core: 2. Of those that a mesh axis runs over, the one named last changes fastest.
Arguments:
- queries: bfloat16 [57344, 4096], P('seq', 'head'), may hold values from -6 to 6
- key_rows: bfloat16 [57344, 4096], P('seq', 'head'), may hold values from -6 to 6
- value_rows: bfloat16 [57344, 4096], P('seq', 'head'), may hold values from -6 to 6
- band_reach: int32 [224], P('seq'), may hold values from 1 to 3, as said below
- far_list: int32 [224, 2], P('seq'), may hold values from 0 to 223, as said below
- slopes: float32 [32], P('head'), may hold values from 1e-05 to 0.08
Outputs:
- mixed: bfloat16 [57344, 4096], P(('seq', 'head'))
The draws below stay inside these ranges and needn't reach their ends.
Inputs may be any that keep to these rules, and one draw needn't show every extreme that they name: Some query block has band_reach exactly 3. `far_list`: block g lies on index g // 14 of seq. Of the 28 far blocks listed for the query blocks of one index of seq, at most 2 lie on any one index, and exactly 2 on some index.
All inputs are finite; a program needn't handle non-finite values.
Results may differ from the reference program's by a relative error of at most 0.0049.
Values may be sent and summed in bfloat16 or wider, within the bound.
No kernel may reach another device: no remote copies, remote signals or barrier semaphores. Data moves between devices by JAX's collectives and lax.ppermute only.
A program may use at most 128 MiB of HBM per device.

```python
import math
import jax
import jax.numpy as jnp
from jax import lax

H = 32
DH = 128
BT = 256
BAND = 3
FAR = 2
BLK_DEV = 14
NBLK = 224
NTOK = 57344
CAP = 2


def drawn(key):
    total_rows = NBLK * BT
    channels = H * DH
    coins = jax.random.randint(jax.random.fold_in(key, 7), (total_rows, channels), 0, 2)
    sign_pattern = (2 * coins - 1).astype(jnp.float32)
    return sign_pattern


def draw_queries(key, part):
    sign_pattern = drawn(key)
    base_draw = jnp.clip(jax.random.normal(jax.random.fold_in(key, 1), sign_pattern.shape, jnp.float32), -6.0, 6.0)
    return base_draw.astype(jnp.bfloat16)


def draw_key_rows(key, part):
    sign_pattern = drawn(key)
    base_draw = jnp.clip(jax.random.normal(jax.random.fold_in(key, 2), sign_pattern.shape, jnp.float32), -6.0, 6.0)
    return base_draw.astype(jnp.bfloat16)


def draw_band_reach(key, part):
    widths = jax.random.randint(jax.random.fold_in(key, 31), (NBLK,), 1, BAND + 1)
    widest = jax.random.randint(jax.random.fold_in(key, 32), (), 0, NBLK)
    return widths.at[widest].set(BAND).astype(jnp.int32)


def far_one_device(device_key):
    device_count = NBLK // BLK_DEV
    request_count = BLK_DEV * FAR
    slot_total = device_count * CAP
    key_heavy, key_order, key_mix, key_local = jax.random.split(device_key, 4)
    heavy = jax.random.randint(key_heavy, (), 0, device_count)
    slot_ids = jnp.arange(slot_total, dtype=jnp.int32)
    slot_source = slot_ids // CAP
    ranking = jax.random.randint(key_order, (slot_total,), 0, 1 << 20) * slot_total + slot_ids
    ranking = jnp.where(slot_source == heavy, slot_ids - 2 * slot_total, ranking)
    order = jnp.argsort(ranking)
    sources = slot_source[order][:request_count]
    mixing = jnp.argsort(jax.random.randint(key_mix, (request_count,), 0, 1 << 20) * request_count + jnp.arange(request_count, dtype=jnp.int32))
    sources = sources[mixing]
    local_blocks = jax.random.randint(key_local, (request_count,), 0, BLK_DEV)
    return (sources * BLK_DEV + local_blocks).reshape(BLK_DEV, FAR)


def draw_far_list(key, part):
    device_count = NBLK // BLK_DEV
    device_keys = jax.random.split(jax.random.fold_in(key, 41), device_count)
    lists = jax.vmap(far_one_device)(device_keys)
    return lists.reshape(NBLK, FAR).astype(jnp.int32)


def levels(stream_key, dims, cuts, smallest, high):
    level, own = 1.0, jax.random.fold_in(stream_key, 6)
    for position, blocks in cuts:
        steps = jnp.exp(jax.random.uniform(jax.random.fold_in(own, position), (blocks,), jnp.float32, smallest / len(cuts), high / len(cuts)))
        level = level * jnp.repeat(steps, dims[position] // blocks).reshape([-1 if axis == position else 1 for axis in range(len(dims))])
    return level


def centred(rng, dims, deviation, bound, cuts=(), kind=jnp.bfloat16):
    values = jax.random.normal(rng, dims, jnp.float32) * deviation
    if len(cuts) > 0:
        values = levels(rng, dims, cuts, -0.22, 0.18) * values
    return jnp.clip(values, min=-bound, max=bound).astype(kind)


def setup_inputs(seed: int = 0) -> dict:
    splits = jax.random.split(jax.random.key(seed), 7)
    queries = draw_queries(jax.random.fold_in(splits[6], 71), 0)
    key_rows = draw_key_rows(jax.random.fold_in(splits[6], 71), 0)
    value_rows = centred(splits[2], (NTOK, H * DH), 1.0, 6.0, ((0, 16), (1, 16)))
    band_reach = draw_band_reach(jax.random.fold_in(splits[6], 71), 0)
    far_list = draw_far_list(jax.random.fold_in(splits[6], 71), 0)
    slopes = jnp.clip(jnp.exp(math.log(0.08) - 8.987197 * jax.random.uniform(splits[5], (H,), jnp.float32) ** levels(splits[5], (H,), ((0, 16),), -0.2, 0.2)), 9.999999747378752e-06, 0.08)
    return {"queries": queries, "key_rows": key_rows, "value_rows": value_rows, "band_reach": band_reach, "far_list": far_list, "slopes": slopes}


def block_attention(query_rows, key_part, value_part, key_pos, key_mask, query_pos, slopes):
    head_count = slopes.shape[0]
    head_size = query_rows.shape[1] // head_count
    queries_h = query_rows.astype(jnp.float32).reshape(query_rows.shape[0], head_count, head_size)
    keys_h = key_part.astype(jnp.float32).reshape(key_part.shape[0], head_count, head_size)
    values_h = value_part.astype(jnp.float32).reshape(value_part.shape[0], head_count, head_size)
    scores = jnp.einsum('qhd,khd->hqk', queries_h, keys_h) * (1.0 / math.sqrt(head_size))
    distance = jnp.abs(query_pos[:, None] - key_pos[None, :]).astype(jnp.float32)
    scores = scores - slopes[:, None, None] * distance[None, :, :]
    scores = jnp.where(key_mask[None, None, :], scores, -jnp.inf)
    row_max = lax.optimization_barrier(jnp.max(scores, axis=2, keepdims=True))
    raised = jnp.exp(scores - row_max)
    weights = (raised / lax.optimization_barrier(jnp.sum(raised, axis=2, keepdims=True))).astype(jnp.bfloat16)
    attended = jnp.einsum('hqk,khd->qhd', weights.astype(jnp.float32), values_h)
    return attended.astype(jnp.bfloat16).reshape(query_rows.shape[0], head_count * head_size)

def reference(queries, key_rows, value_rows, band_reach, far_list, slopes):
    total_tokens, channels = key_rows.shape
    total_blocks = total_tokens // BT
    margin = BAND * BT
    band_span = 2 * BAND + 1
    keys_pad = jnp.pad(key_rows, ((margin, margin), (0, 0)))
    values_pad = jnp.pad(value_rows, ((margin, margin), (0, 0)))
    offsets = jnp.arange(band_span, dtype=jnp.int32) - BAND
    within = jnp.arange(BT, dtype=jnp.int32)

    def attend(block_id):
        first_row = block_id * BT
        band_keys = lax.dynamic_slice_in_dim(keys_pad, first_row, band_span * BT, 0)
        band_values = lax.dynamic_slice_in_dim(values_pad, first_row, band_span * BT, 0)
        far_here = far_list[block_id]
        far_keys = jnp.concatenate([lax.dynamic_slice_in_dim(key_rows, (far_here[far_slot] * BT).astype(jnp.int32), BT, 0) for far_slot in range(FAR)], axis=0)
        far_values = jnp.concatenate([lax.dynamic_slice_in_dim(value_rows, (far_here[far_slot] * BT).astype(jnp.int32), BT, 0) for far_slot in range(FAR)], axis=0)
        band_blocks = block_id + offsets
        band_ok = (jnp.abs(offsets) <= band_reach[block_id]) & (band_blocks >= 0) & (band_blocks < total_blocks)
        key_blocks = jnp.concatenate([band_blocks, far_here.astype(jnp.int32)])
        key_ok = jnp.concatenate([band_ok, jnp.ones((FAR,), jnp.bool_)])
        key_pos = (key_blocks[:, None] * BT + within[None, :]).reshape(-1)
        key_mask = jnp.repeat(key_ok, BT)
        query_rows = lax.dynamic_slice_in_dim(queries, first_row, BT, 0)
        return block_attention(query_rows, jnp.concatenate([band_keys, far_keys], axis=0), jnp.concatenate([band_values, far_values], axis=0), key_pos, key_mask, first_row + within, slopes)
    attended = lax.map(attend, jnp.arange(total_blocks, dtype=jnp.int32))
    return attended.reshape(total_tokens, channels)
```

```python
import functools
import math

import jax
import jax.numpy as jnp
from jax import lax
from jax.experimental import pallas as pl
from jax.experimental.pallas import tpu as pltpu
from jax.sharding import PartitionSpec as P


BT = 256
BAND = 3
FAR = 2
CAP = 2
DH = 128
LOG2E = 1.4426950408889634
FAR_AWAY = 1e30
MIB = 1 << 20


def route_kernel(far_ref, table_ref, slot_ref, count_ref, *, sources, blk_dev):
    for s in range(sources):
        count_ref[s] = 0
        for r in range(CAP):
            table_ref[s, r] = 0

    def step(i, carry):
        for f in range(FAR):
            block = far_ref[f, i]
            s = lax.div(block, blk_dev)
            r = jnp.minimum(count_ref[s], CAP - 1)
            count_ref[s] = r + 1
            table_ref[s, r] = block - s * blk_dev
            slot_ref[f, i] = s * CAP + r
        return carry

    lax.fori_loop(0, blk_dev, step, 0)


def route(far_list, sources):
    blk_dev = far_list.shape[0]
    smem = pl.BlockSpec(memory_space=pltpu.SMEM)
    return pl.pallas_call(
        functools.partial(route_kernel, sources=sources, blk_dev=blk_dev),
        out_shape=(
            jax.ShapeDtypeStruct((sources, CAP), jnp.int32),
            jax.ShapeDtypeStruct((FAR, blk_dev), jnp.int32),
        ),
        in_specs=[smem],
        out_specs=(smem, smem),
        scratch_shapes=[pltpu.SMEM((sources,), jnp.int32)],
        name="route",
    )(far_list.T)


def pack_kernel(asked_ref, me_ref, keys_ref, values_ref, *refs, shifts, head):
    out_refs, sems = refs[:-1], refs[-1]
    column = pl.ds(head * DH, DH)
    copies = []
    for shift in range(shifts):
        target = me_ref[0] + shift
        target = jnp.where(target >= shifts, target - shifts, target)
        for r in range(CAP):
            rows = pl.ds(pl.multiple_of(asked_ref[target, r] * BT, BT), BT)
            for which, ref in enumerate((keys_ref, values_ref)):
                slot = r * 2 + which
                if len(out_refs) == 1:
                    dst = out_refs[0].at[target, slot]
                else:
                    dst = out_refs[shift].at[slot]
                copy = pltpu.make_async_copy(ref.at[rows, column], dst, sems.at[shift, slot])
                copy.start()
                copies.append(copy)
    for copy in copies:
        copy.wait()


def pack(asked, me, key_rows, value_rows, head, split):
    shifts = asked.shape[0]
    smem = pl.BlockSpec(memory_space=pltpu.SMEM)
    hbm = pl.BlockSpec(memory_space=pltpu.HBM)
    one = jax.ShapeDtypeStruct((CAP * 2, BT, DH), jnp.bfloat16)
    if split:
        out_shape = (one,) * shifts
    else:
        out_shape = (jax.ShapeDtypeStruct((shifts,) + one.shape, one.dtype),)
    return pl.pallas_call(
        functools.partial(pack_kernel, shifts=shifts, head=head),
        out_shape=out_shape,
        in_specs=[smem, smem, hbm, hbm],
        out_specs=(hbm,) * len(out_shape),
        scratch_shapes=[pltpu.SemaphoreType.DMA((shifts, CAP * 2))],
        name="pack",
    )(asked, me, key_rows, value_rows)


def distances():
    rows = lax.broadcasted_iota(jnp.int32, (BT, BT), 0)
    columns = lax.broadcasted_iota(jnp.int32, (BT, BT), 1)
    return (rows - columns).astype(jnp.float32)


def pair_scores(query, key, offset, slope, gap):
    product = lax.dot_general(
        query, key, (((1,), (1,)), ((), ())), preferred_element_type=jnp.float32
    )
    return product * (LOG2E / math.sqrt(DH)) - slope * jnp.abs(gap + offset)


def weighted(weights, value):
    return lax.dot_general(
        weights.astype(jnp.bfloat16), value, (((1,), (0,)), ((), ())),
        preferred_element_type=jnp.float32,
    )


def row_max(scores):
    return jnp.max(scores, axis=1, keepdims=True)


def row_sum(scores):
    return jnp.sum(scores, axis=1, keepdims=True)


def band_kernel(
    meta_ref, slopes_ref, query_ref, keys_hbm, values_hbm, before_hbm, after_hbm,
    acc_ref, stat_ref,
    keys_ref, values_ref, gap_ref, max_ref, sum_ref, sems, *, blk_dev, total_blocks,
):
    head = pl.program_id(0)
    local = pl.program_id(1)
    margin = BAND * BT
    tok_rows = blk_dev * BT

    @pl.when(local == 0)
    def _():
        column = pl.ds(pl.multiple_of(head * DH, DH), DH)
        copies = []
        for which, (ref, whole) in enumerate(((keys_ref, keys_hbm), (values_ref, values_hbm))):
            copies += [
                pltpu.make_async_copy(
                    before_hbm.at[which, :, column], ref.at[pl.ds(0, margin)], sems.at[which, 0]
                ),
                pltpu.make_async_copy(
                    whole.at[:, column], ref.at[pl.ds(margin, tok_rows)], sems.at[which, 1]
                ),
                pltpu.make_async_copy(
                    after_hbm.at[which, :, column],
                    ref.at[pl.ds(margin + tok_rows, margin)],
                    sems.at[which, 2],
                ),
            ]
        for copy in copies:
            copy.start()
        gap_ref[...] = distances()
        for copy in copies:
            copy.wait()

    slope = slopes_ref[head] * LOG2E
    reach = meta_ref[local]
    block = meta_ref[blk_dev] * blk_dev + local
    query = query_ref[...]

    def rows_of(offset):
        return pl.ds(pl.multiple_of((local + BAND + offset) * BT, BT), BT)

    scores = pair_scores(query, keys_ref[rows_of(0), :], 0.0, slope, gap_ref[...])
    top = row_max(scores)
    weights = jnp.exp2(scores - top)
    max_ref[...] = top
    sum_ref[...] = row_sum(weights)
    acc_ref[...] = weighted(weights, values_ref[rows_of(0), :])

    for distance in range(1, BAND + 1):

        @pl.when(reach >= distance)
        def _():
            low = jnp.where(block >= distance, float(distance * BT), FAR_AWAY)
            high = jnp.where(block + distance < total_blocks, -float(distance * BT), -FAR_AWAY)
            gap = gap_ref[...]
            first = pair_scores(query, keys_ref[rows_of(-distance), :], low, slope, gap)
            second = pair_scores(query, keys_ref[rows_of(distance), :], high, slope, gap)
            old = max_ref[...]
            top = jnp.maximum(old, row_max(jnp.maximum(first, second)))
            shrink = jnp.exp2(old - top)
            first = jnp.exp2(first - top)
            second = jnp.exp2(second - top)
            max_ref[...] = top
            sum_ref[...] = sum_ref[...] * shrink + row_sum(first + second)
            acc_ref[...] = (
                acc_ref[...] * shrink
                + weighted(first, values_ref[rows_of(-distance), :])
                + weighted(second, values_ref[rows_of(distance), :])
            )

    lane = lax.broadcasted_iota(jnp.int32, (BT, DH), 1)
    stat_ref[...] = jnp.where(lane < DH // 2, max_ref[...], sum_ref[...])


def band_attention(meta, slopes, queries, key_rows, value_rows, before, after, total_blocks):
    tok_rows, channels = queries.shape
    blk_dev = tok_rows // BT
    heads = channels // DH
    any_spec = pl.BlockSpec(memory_space=pltpu.HBM)
    tile = pl.BlockSpec((BT, DH), lambda h, i, *_: (i, h))
    ext = tok_rows + 2 * BAND * BT
    return pl.pallas_call(
        functools.partial(band_kernel, blk_dev=blk_dev, total_blocks=total_blocks),
        out_shape=(
            jax.ShapeDtypeStruct((tok_rows, channels), jnp.float32),
            jax.ShapeDtypeStruct((tok_rows, channels), jnp.float32),
        ),
        grid_spec=pltpu.PrefetchScalarGridSpec(
            num_scalar_prefetch=2,
            grid=(heads, blk_dev),
            in_specs=[tile, any_spec, any_spec, any_spec, any_spec],
            out_specs=(tile, tile),
            scratch_shapes=[
                pltpu.VMEM((ext, DH), jnp.bfloat16),
                pltpu.VMEM((ext, DH), jnp.bfloat16),
                pltpu.VMEM((BT, BT), jnp.float32),
                pltpu.VMEM((BT, 1), jnp.float32),
                pltpu.VMEM((BT, 1), jnp.float32),
                pltpu.SemaphoreType.DMA((2, 3)),
            ],
        ),
        compiler_params=pltpu.CompilerParams(vmem_limit_bytes=24 * MIB),
        cost_estimate=pl.CostEstimate(
            flops=7 * 4 * tok_rows * BT * channels,
            transcendentals=7 * tok_rows * BT * heads,
            bytes_accessed=30 * MIB,
        ),
        name="band",
    )(meta, slopes, queries, key_rows, value_rows, before, after)


def far_kernel(
    meta_ref, slot_ref, block_ref, slopes_ref, query_ref, acc_ref, stat_ref, *refs, head, blk_dev,
    sources,
):
    pieces = refs[:-4]
    out_ref, buffer_ref, gap_ref, sems = refs[-4:]
    local = pl.program_id(0)

    @pl.when(local == 0)
    def _():
        if len(pieces) == 1:
            copies = [
                pltpu.make_async_copy(pieces[0].at[s], buffer_ref.at[s], sems.at[s])
                for s in range(sources)
            ]
        else:
            copies = [
                pltpu.make_async_copy(piece, buffer_ref.at[s], sems.at[s])
                for s, piece in enumerate(pieces)
            ]
        for copy in copies:
            copy.start()
        gap_ref[...] = distances()
        for copy in copies:
            copy.wait()

    slope = slopes_ref[head] * LOG2E
    me = meta_ref[blk_dev]
    block = me * blk_dev + local
    query = query_ref[...]
    gap = gap_ref[...]
    scores = []
    values = []
    for f in range(FAR):
        offset = ((block - block_ref[f, local]) * BT).astype(jnp.float32)
        slot = slot_ref[f, local]
        source = lax.div(slot, CAP)
        if len(pieces) > 1:
            source = me - source
            source = jnp.where(source < 0, source + sources, source)
        rank = lax.rem(slot, CAP)
        scores.append(pair_scores(query, buffer_ref[source, rank * 2], offset, slope, gap))
        values.append(buffer_ref[source, rank * 2 + 1])
    old = stat_ref[:, 0:1]
    old_sum = stat_ref[:, DH // 2 : DH // 2 + 1]
    top = jnp.maximum(old, row_max(jnp.maximum(scores[0], scores[1])))
    shrink = jnp.exp2(old - top)
    first = jnp.exp2(scores[0] - top)
    second = jnp.exp2(scores[1] - top)
    total = old_sum * shrink + row_sum(first + second)
    acc = acc_ref[...] * shrink + weighted(first, values[0]) + weighted(second, values[1])
    out_ref[...] = (acc / total).astype(jnp.bfloat16)


def far_attention(meta, slots, far_blocks, slopes, queries, acc, stat, pieces, head, sources):
    tok_rows = queries.shape[0]
    blk_dev = tok_rows // BT
    tile = pl.BlockSpec((BT, DH), lambda i, *_: (i, head))
    any_spec = pl.BlockSpec(memory_space=pltpu.HBM)
    return pl.pallas_call(
        functools.partial(far_kernel, head=head, blk_dev=blk_dev, sources=sources),
        out_shape=jax.ShapeDtypeStruct((tok_rows, DH), jnp.bfloat16),
        grid_spec=pltpu.PrefetchScalarGridSpec(
            num_scalar_prefetch=4,
            grid=(blk_dev,),
            in_specs=[tile, tile, tile] + [any_spec] * len(pieces),
            out_specs=pl.BlockSpec((BT, DH), lambda i, *_: (i, 0)),
            scratch_shapes=[
                pltpu.VMEM((sources, CAP * 2, BT, DH), jnp.bfloat16),
                pltpu.VMEM((BT, BT), jnp.float32),
                pltpu.SemaphoreType.DMA((sources,)),
            ],
        ),
        compiler_params=pltpu.CompilerParams(vmem_limit_bytes=16 * MIB),
        cost_estimate=pl.CostEstimate(
            flops=2 * 4 * tok_rows * BT * DH,
            transcendentals=2 * tok_rows * BT,
            bytes_accessed=14 * MIB,
        ),
        name="far",
    )(meta, slots, far_blocks, slopes, queries, acc, stat, *pieces)


def body(queries, key_rows, value_rows, band_reach, far_list, slopes):
    myself = lax.axis_index("seq")
    sources = lax.axis_size("seq")
    tok_rows, channels = key_rows.shape
    blk_dev = tok_rows // BT
    margin = BAND * BT
    heads = channels // DH
    up = [(i, i + 1) for i in range(sources - 1)]
    down = [(i + 1, i) for i in range(sources - 1)]

    table, slots = route(far_list, sources)
    asked = lax.all_to_all(table, "seq", split_axis=0, concat_axis=0, tiled=True)
    last = jnp.stack([key_rows[tok_rows - margin :], value_rows[tok_rows - margin :]])
    first = jnp.stack([key_rows[:margin], value_rows[:margin]])
    before = lax.ppermute(last, "seq", up)
    after = lax.ppermute(first, "seq", down)

    me = myself[None].astype(jnp.int32)
    incoming = []
    for head in range(heads):
        split = head == heads - 1
        outgoing = pack(asked, me, key_rows, value_rows, head, split)
        if split:
            pieces = [outgoing[0]]
            for shift in range(1, sources):
                ring = [(i, (i + shift) % sources) for i in range(sources)]
                pieces.append(lax.ppermute(outgoing[shift], "seq", ring))
            incoming.append(pieces)
        else:
            incoming.append(
                [lax.all_to_all(outgoing[0], "seq", split_axis=0, concat_axis=0, tiled=True)]
            )

    meta = jnp.concatenate([band_reach, me])
    acc, stat = band_attention(
        meta, slopes, queries, key_rows, value_rows, before, after, blk_dev * sources
    )
    acc, stat, queries = (
        pltpu.with_memory_space_constraint(x, pltpu.HBM) for x in (acc, stat, queries)
    )
    parts = []
    for head in range(heads):
        attended = far_attention(
            meta, slots, far_list.T, slopes, queries, acc, stat, incoming[head], head, sources
        )
        parts.append(
            lax.all_to_all(
                attended.reshape(lax.axis_size("head"), -1, DH), "head",
                split_axis=0, concat_axis=0, tiled=True,
            )
        )
    mixed = jnp.stack(parts, axis=1)
    return mixed.transpose(2, 0, 1, 3).reshape(mixed.shape[2], -1)


def solution(mesh):
    in_specs = (
        P("seq", "head"),
        P("seq", "head"),
        P("seq", "head"),
        P("seq"),
        P("seq", None),
        P("head"),
    )
    out_specs = P(("seq", "head"), None)

    return jax.shard_map(body, mesh=mesh, in_specs=in_specs, out_specs=out_specs, check_vma=False)
```

```python
import functools
import math

import jax
import jax.numpy as jnp
from jax import lax
from jax.experimental import pallas as pl
from jax.experimental.pallas import tpu as pltpu
from jax.sharding import PartitionSpec as P


BT = 256
BAND = 3
FAR = 2
CAP = 2
DH = 128
LOG2E = 1.4426950408889634
FAR_AWAY = 1e30
MIB = 1 << 20


def route_kernel(far_ref, table_ref, slot_ref, count_ref, *, sources, blk_dev):
    for s in range(sources):
        count_ref[s] = 0
        for r in range(CAP):
            table_ref[s, r] = 0

    def step(i, carry):
        for f in range(FAR):
            block = far_ref[f, i]
            s = lax.div(block, blk_dev)
            r = jnp.minimum(count_ref[s], CAP - 1)
            count_ref[s] = r + 1
            table_ref[s, r] = block - s * blk_dev
            slot_ref[f, i] = s * CAP + r
        return carry

    lax.fori_loop(0, blk_dev, step, 0)


def route(far_list, sources):
    blk_dev = far_list.shape[0]
    smem = pl.BlockSpec(memory_space=pltpu.SMEM)
    return pl.pallas_call(
        functools.partial(route_kernel, sources=sources, blk_dev=blk_dev),
        out_shape=(
            jax.ShapeDtypeStruct((sources, CAP), jnp.int32),
            jax.ShapeDtypeStruct((FAR, blk_dev), jnp.int32),
        ),
        in_specs=[smem],
        out_specs=(smem, smem),
        scratch_shapes=[pltpu.SMEM((sources,), jnp.int32)],
        name="route",
    )(far_list.T)


def pack_kernel(asked_ref, me_ref, keys_ref, values_ref, *refs, shifts):
    out_refs, sems = refs[:-1], refs[-1]
    copies = []
    for shift in range(shifts):
        target = me_ref[0] + shift
        target = jnp.where(target >= shifts, target - shifts, target)
        for r in range(CAP):
            rows = pl.ds(pl.multiple_of(asked_ref[target, r] * BT, BT), BT)
            for which, ref in enumerate((keys_ref, values_ref)):
                slot = r * 2 + which
                if len(out_refs) == 1:
                    dst = out_refs[0].at[target, slot]
                else:
                    dst = out_refs[shift].at[slot]
                copy = pltpu.make_async_copy(ref.at[rows, :], dst, sems.at[shift, slot])
                copy.start()
                copies.append(copy)
    for copy in copies:
        copy.wait()


def pack(asked, me, key_rows, value_rows, head, split):
    shifts = asked.shape[0]
    tok_rows = key_rows.shape[0]
    hbm = pl.BlockSpec(memory_space=pltpu.HBM)
    column = pl.BlockSpec((tok_rows, DH), lambda i, *_: (0, head))
    one = (CAP * 2, BT, DH)
    if split:
        out_shape = (pltpu.HBM(one, key_rows.dtype),) * shifts
    else:
        out_shape = (pltpu.HBM((shifts,) + one, key_rows.dtype),)
    return pl.pallas_call(
        functools.partial(pack_kernel, shifts=shifts),
        out_shape=out_shape,
        grid_spec=pltpu.PrefetchScalarGridSpec(
            num_scalar_prefetch=2,
            grid=(1,),
            in_specs=[column, column],
            out_specs=(hbm,) * len(out_shape),
            scratch_shapes=[pltpu.SemaphoreType.DMA((shifts, CAP * 2))],
        ),
        compiler_params=pltpu.CompilerParams(vmem_limit_bytes=16 * MIB),
        name="pack",
    )(asked, me, key_rows, value_rows)


def distances():
    rows = lax.broadcasted_iota(jnp.int32, (BT, BT), 0)
    columns = lax.broadcasted_iota(jnp.int32, (BT, BT), 1)
    return (rows - columns).astype(jnp.float32)


def pair_scores(query, key, offset, slope, gap):
    product = lax.dot_general(
        query, key, (((1,), (1,)), ((), ())), preferred_element_type=jnp.float32
    )
    return product * (LOG2E / math.sqrt(DH)) - slope * jnp.abs(gap + offset)


def weighted(weights, value):
    return lax.dot_general(
        weights.astype(jnp.bfloat16), value, (((1,), (0,)), ((), ())),
        preferred_element_type=jnp.float32,
    )


def row_max(scores):
    return jnp.max(scores, axis=1, keepdims=True)


def row_sum(scores):
    return jnp.sum(scores, axis=1, keepdims=True)


def band_kernel(
    meta_ref, slopes_ref, query_ref, keys_hbm, values_hbm, before_hbm, after_hbm,
    acc_ref, stat_ref,
    keys_ref, values_ref, gap_ref, max_ref, sum_ref, sems, *, blk_dev, total_blocks,
):
    head = pl.program_id(0)
    local = pl.program_id(1)
    margin = BAND * BT
    tok_rows = blk_dev * BT

    @pl.when(local == 0)
    def _():
        column = pl.ds(pl.multiple_of(head * DH, DH), DH)
        copies = []
        for which, (ref, whole) in enumerate(((keys_ref, keys_hbm), (values_ref, values_hbm))):
            copies += [
                pltpu.make_async_copy(
                    before_hbm.at[which, :, column], ref.at[pl.ds(0, margin)], sems.at[which, 0]
                ),
                pltpu.make_async_copy(
                    whole.at[:, column], ref.at[pl.ds(margin, tok_rows)], sems.at[which, 1]
                ),
                pltpu.make_async_copy(
                    after_hbm.at[which, :, column],
                    ref.at[pl.ds(margin + tok_rows, margin)],
                    sems.at[which, 2],
                ),
            ]
        for copy in copies:
            copy.start()
        gap_ref[...] = distances()
        for copy in copies:
            copy.wait()

    slope = slopes_ref[head] * LOG2E
    reach = meta_ref[local]
    block = meta_ref[blk_dev] * blk_dev + local
    query = query_ref[...]

    def rows_of(offset):
        return pl.ds(pl.multiple_of((local + BAND + offset) * BT, BT), BT)

    scores = pair_scores(query, keys_ref[rows_of(0), :], 0.0, slope, gap_ref[...])
    top = row_max(scores)
    weights = jnp.exp2(scores - top)
    max_ref[...] = top
    sum_ref[...] = row_sum(weights)
    acc_ref[...] = weighted(weights, values_ref[rows_of(0), :])

    for distance in range(1, BAND + 1):

        @pl.when(reach >= distance)
        def _():
            low = jnp.where(block >= distance, float(distance * BT), FAR_AWAY)
            high = jnp.where(block + distance < total_blocks, -float(distance * BT), -FAR_AWAY)
            gap = gap_ref[...]
            first = pair_scores(query, keys_ref[rows_of(-distance), :], low, slope, gap)
            second = pair_scores(query, keys_ref[rows_of(distance), :], high, slope, gap)
            old = max_ref[...]
            top = jnp.maximum(old, row_max(jnp.maximum(first, second)))
            shrink = jnp.exp2(old - top)
            first = jnp.exp2(first - top)
            second = jnp.exp2(second - top)
            max_ref[...] = top
            sum_ref[...] = sum_ref[...] * shrink + row_sum(first + second)
            acc_ref[...] = (
                acc_ref[...] * shrink
                + weighted(first, values_ref[rows_of(-distance), :])
                + weighted(second, values_ref[rows_of(distance), :])
            )

    total = sum_ref[...]
    acc_ref[...] = acc_ref[...] / total
    stat_ref[...] = jnp.broadcast_to(max_ref[...] + jnp.log2(total), (BT, DH))


def band_attention(meta, slopes, queries, key_rows, value_rows, before, after, total_blocks):
    tok_rows, channels = queries.shape
    blk_dev = tok_rows // BT
    heads = channels // DH
    any_spec = pl.BlockSpec(memory_space=pltpu.HBM)
    tile = pl.BlockSpec((BT, DH), lambda h, i, *_: (i, h))
    ext = tok_rows + 2 * BAND * BT
    return pl.pallas_call(
        functools.partial(band_kernel, blk_dev=blk_dev, total_blocks=total_blocks),
        out_shape=(
            jax.ShapeDtypeStruct((tok_rows, channels), jnp.float32),
            jax.ShapeDtypeStruct((tok_rows, channels), jnp.float32),
        ),
        grid_spec=pltpu.PrefetchScalarGridSpec(
            num_scalar_prefetch=2,
            grid=(heads, blk_dev),
            in_specs=[tile, any_spec, any_spec, any_spec, any_spec],
            out_specs=(tile, tile),
            scratch_shapes=[
                pltpu.VMEM((ext, DH), jnp.bfloat16),
                pltpu.VMEM((ext, DH), jnp.bfloat16),
                pltpu.VMEM((BT, BT), jnp.float32),
                pltpu.VMEM((BT, 1), jnp.float32),
                pltpu.VMEM((BT, 1), jnp.float32),
                pltpu.SemaphoreType.DMA((2, 3)),
            ],
        ),
        compiler_params=pltpu.CompilerParams(vmem_limit_bytes=24 * MIB),
        cost_estimate=pl.CostEstimate(
            flops=7 * 4 * tok_rows * BT * channels,
            transcendentals=7 * tok_rows * BT * heads,
            bytes_accessed=30 * MIB,
        ),
        name="band",
    )(meta, slopes, queries, key_rows, value_rows, before, after)


def far_kernel(
    meta_ref, slot_ref, block_ref, slopes_ref, query_ref, acc_ref, stat_ref, *refs, head, blk_dev,
    sources, group,
):
    pieces = refs[:-4]
    out_ref, buffer_ref, gap_ref, sems = refs[-4:]
    local = pl.program_id(0)

    @pl.when(local == 0)
    def _():
        if len(pieces) == 1:
            copies = [
                pltpu.make_async_copy(pieces[0].at[s], buffer_ref.at[s], sems.at[s])
                for s in range(sources)
            ]
        else:
            copies = [
                pltpu.make_async_copy(piece, buffer_ref.at[s], sems.at[s])
                for s, piece in enumerate(pieces)
            ]
        for copy in copies:
            copy.start()
        gap_ref[...] = distances()
        for copy in copies:
            copy.wait()

    slope = slopes_ref[head] * LOG2E
    me = meta_ref[blk_dev]
    gap = gap_ref[...]
    ones = jnp.ones((BT, DH), jnp.bfloat16)
    for part in range(group):
        i = local * group + part
        rows = pl.ds(part * BT, BT)
        block = me * blk_dev + i
        query = query_ref[rows, :]
        scores = []
        values = []
        for f in range(FAR):
            offset = ((block - block_ref[f, i]) * BT).astype(jnp.float32)
            slot = slot_ref[f, i]
            source = lax.div(slot, CAP)
            if len(pieces) > 1:
                source = me - source
                source = jnp.where(source < 0, source + sources, source)
            rank = lax.rem(slot, CAP)
            scores.append(pair_scores(query, buffer_ref[source, rank * 2], offset, slope, gap))
            values.append(jnp.concatenate([buffer_ref[source, rank * 2 + 1], ones], axis=1))
        band = stat_ref[rows, :]
        top = jnp.maximum(band[:, 0:1], row_max(jnp.maximum(scores[0], scores[1])))
        weights = [jnp.exp2(score - top) for score in scores]
        far = weighted(weights[0], values[0]) + weighted(weights[1], values[1])
        share = jnp.exp2(band - top)
        acc = acc_ref[rows, :] * share + far[:, :DH]
        out_ref[rows, :] = (acc / (share + far[:, DH:])).astype(jnp.bfloat16)


def far_attention(meta, slots, far_blocks, slopes, queries, acc, stat, pieces, head, sources):
    tok_rows = queries.shape[0]
    blk_dev = tok_rows // BT
    group = 2 if blk_dev % 2 == 0 else 1
    tile = pl.BlockSpec((group * BT, DH), lambda i, *_: (i, head))
    hbm = pl.BlockSpec(memory_space=pltpu.HBM)
    return pl.pallas_call(
        functools.partial(far_kernel, head=head, blk_dev=blk_dev, sources=sources, group=group),
        out_shape=jax.ShapeDtypeStruct((tok_rows, DH), jnp.bfloat16),
        grid_spec=pltpu.PrefetchScalarGridSpec(
            num_scalar_prefetch=4,
            grid=(blk_dev // group,),
            in_specs=[tile, tile, tile] + [hbm] * len(pieces),
            out_specs=pl.BlockSpec((group * BT, DH), lambda i, *_: (i, 0)),
            scratch_shapes=[
                pltpu.VMEM((sources, CAP * 2, BT, DH), jnp.bfloat16),
                pltpu.VMEM((BT, BT), jnp.float32),
                pltpu.SemaphoreType.DMA((sources,)),
            ],
        ),
        compiler_params=pltpu.CompilerParams(vmem_limit_bytes=16 * MIB),
        cost_estimate=pl.CostEstimate(
            flops=2 * 4 * tok_rows * BT * DH,
            transcendentals=2 * tok_rows * BT,
            bytes_accessed=14 * MIB,
        ),
        name="far",
    )(meta, slots, far_blocks, slopes, queries, acc, stat, *pieces)


def place_kernel(part_ref, *refs, head):
    out_ref, buffer_ref, in_sems, out_sems = refs[-4:]
    peers = part_ref.shape[0]
    width = out_ref.shape[1] // peers
    loads = [
        pltpu.make_async_copy(part_ref.at[g], buffer_ref.at[g], in_sems.at[g])
        for g in range(peers)
    ]
    stores = [
        pltpu.make_async_copy(
            buffer_ref.at[g], out_ref.at[:, pl.ds(g * width + head * DH, DH)], out_sems.at[g]
        )
        for g in range(peers)
    ]
    for load in loads:
        load.start()
    for load, store in zip(loads, stores):
        load.wait()
        store.start()
    for store in stores:
        store.wait()


def place(part, so_far, head, heads):
    peers, rows, _ = part.shape
    hbm = pl.BlockSpec(memory_space=pltpu.HBM)
    args = (part,) if so_far is None else (part, so_far)
    return pl.pallas_call(
        functools.partial(place_kernel, head=head),
        out_shape=jax.ShapeDtypeStruct((rows, peers * heads * DH), part.dtype),
        in_specs=[hbm] * len(args),
        out_specs=hbm,
        scratch_shapes=[
            pltpu.VMEM(part.shape, part.dtype),
            pltpu.SemaphoreType.DMA((peers,)),
            pltpu.SemaphoreType.DMA((peers,)),
        ],
        input_output_aliases={} if so_far is None else {1: 0},
        name="place",
    )(*args)


def body(queries, key_rows, value_rows, band_reach, far_list, slopes):
    myself = lax.axis_index("seq")
    sources = lax.axis_size("seq")
    tok_rows, channels = key_rows.shape
    blk_dev = tok_rows // BT
    margin = BAND * BT
    heads = channels // DH
    up = [(i, i + 1) for i in range(sources - 1)]
    down = [(i + 1, i) for i in range(sources - 1)]

    table, slots = route(far_list, sources)
    asked = lax.all_to_all(table, "seq", split_axis=0, concat_axis=0, tiled=True)
    last = jnp.stack([key_rows[tok_rows - margin :], value_rows[tok_rows - margin :]])
    first = jnp.stack([key_rows[:margin], value_rows[:margin]])
    before = lax.ppermute(last, "seq", up)
    after = lax.ppermute(first, "seq", down)

    me = myself[None].astype(jnp.int32)
    keys_hbm, values_hbm = (
        pltpu.with_memory_space_constraint(x, pltpu.HBM) for x in (key_rows, value_rows)
    )
    incoming = []
    for head in range(heads):
        split = head == heads - 1
        outgoing = pack(asked, me, keys_hbm, values_hbm, head, split)
        if split:
            pieces = [outgoing[0]]
            for shift in range(1, sources):
                ring = [(i, (i + shift) % sources) for i in range(sources)]
                pieces.append(lax.ppermute(outgoing[shift], "seq", ring))
            incoming.append(pieces)
        else:
            incoming.append(
                [lax.all_to_all(outgoing[0], "seq", split_axis=0, concat_axis=0, tiled=True)]
            )

    meta = jnp.concatenate([band_reach, me])
    acc, stat = band_attention(
        meta, slopes, queries, key_rows, value_rows, before, after, blk_dev * sources
    )
    acc, stat, queries = (
        pltpu.with_memory_space_constraint(x, pltpu.HBM) for x in (acc, stat, queries)
    )
    mixed = None
    for head in range(heads):
        attended = far_attention(
            meta, slots, far_list.T, slopes, queries, acc, stat, incoming[head], head, sources
        )
        part = lax.all_to_all(
            attended.reshape(lax.axis_size("head"), -1, DH), "head",
            split_axis=0, concat_axis=0, tiled=True,
        )
        mixed = place(part, mixed, head, heads)
    return mixed


def solution(mesh):
    in_specs = (
        P("seq", "head"),
        P("seq", "head"),
        P("seq", "head"),
        P("seq"),
        P("seq", None),
        P("head"),
    )
    out_specs = P(("seq", "head"), None)

    return jax.shard_map(body, mesh=mesh, in_specs=in_specs, out_specs=out_specs, check_vma=False)
```

```python
import functools
import math

import jax
import jax.numpy as jnp
from jax import lax
from jax.experimental import pallas as pl
from jax.experimental.pallas import tpu as pltpu
from jax.sharding import PartitionSpec as P


BT = 256
BAND = 3
FAR = 2
CAP = 2
DH = 128
LOG2E = 1.4426950408889634
FAR_AWAY = 1e30
MIB = 1 << 20


def route_kernel(far_ref, table_ref, slot_ref, count_ref, *, sources, blk_dev):
    for s in range(sources):
        count_ref[s] = 0
        for r in range(CAP):
            table_ref[s, r] = 0

    def step(i, carry):
        for f in range(FAR):
            block = far_ref[f, i]
            s = lax.div(block, blk_dev)
            r = jnp.minimum(count_ref[s], CAP - 1)
            count_ref[s] = r + 1
            table_ref[s, r] = block - s * blk_dev
            slot_ref[f, i] = s * CAP + r
        return carry

    lax.fori_loop(0, blk_dev, step, 0)


def route(far_list, sources):
    blk_dev = far_list.shape[0]
    smem = pl.BlockSpec(memory_space=pltpu.SMEM)
    return pl.pallas_call(
        functools.partial(route_kernel, sources=sources, blk_dev=blk_dev),
        out_shape=(
            jax.ShapeDtypeStruct((sources, CAP), jnp.int32),
            jax.ShapeDtypeStruct((FAR, blk_dev), jnp.int32),
        ),
        in_specs=[smem],
        out_specs=(smem, smem),
        scratch_shapes=[pltpu.SMEM((sources,), jnp.int32)],
        name="route",
    )(far_list.T)


def pack_kernel(asked_ref, me_ref, keys_ref, values_ref, *refs, shifts):
    out_refs, sems = refs[:-1], refs[-1]
    copies = []
    for which, ref in enumerate((keys_ref, values_ref)):
        for shift in range(shifts):
            target = me_ref[0] + shift
            target = jnp.where(target >= shifts, target - shifts, target)
            for r in range(CAP):
                rows = pl.ds(pl.multiple_of(asked_ref[target, r] * BT, BT), BT)
                slot = r * 2 + which
                if len(out_refs) == 1:
                    dst = out_refs[0].at[target, slot]
                else:
                    dst = out_refs[which * shifts + shift].at[r]
                copy = pltpu.make_async_copy(ref.at[rows, :], dst, sems.at[shift, slot])
                copy.start()
                copies.append(copy)
    for copy in copies:
        copy.wait()


def pack(asked, me, key_rows, value_rows, head, split):
    shifts = asked.shape[0]
    tok_rows = key_rows.shape[0]
    hbm = pl.BlockSpec(memory_space=pltpu.HBM)
    column = pl.BlockSpec((tok_rows, DH), lambda i, *_: (0, head))
    if split:
        out_shape = (pltpu.HBM((CAP, BT, DH), key_rows.dtype),) * (2 * shifts)
    else:
        out_shape = (pltpu.HBM((shifts, CAP * 2, BT, DH), key_rows.dtype),)
    return pl.pallas_call(
        functools.partial(pack_kernel, shifts=shifts),
        out_shape=out_shape,
        grid_spec=pltpu.PrefetchScalarGridSpec(
            num_scalar_prefetch=2,
            grid=(1,),
            in_specs=[column, column],
            out_specs=(hbm,) * len(out_shape),
            scratch_shapes=[pltpu.SemaphoreType.DMA((shifts, CAP * 2))],
        ),
        compiler_params=pltpu.CompilerParams(vmem_limit_bytes=16 * MIB),
        name="pack",
    )(asked, me, key_rows, value_rows)


def distances():
    rows = lax.broadcasted_iota(jnp.int32, (BT, BT), 0)
    columns = lax.broadcasted_iota(jnp.int32, (BT, BT), 1)
    return (rows - columns).astype(jnp.float32)


def pair_scores(query, key, offset, slope, gap):
    product = lax.dot_general(
        query, key, (((1,), (1,)), ((), ())), preferred_element_type=jnp.float32
    )
    return product * (LOG2E / math.sqrt(DH)) - slope * jnp.abs(gap + offset)


def weighted(weights, value):
    return lax.dot_general(
        weights.astype(jnp.bfloat16), value, (((1,), (0,)), ((), ())),
        preferred_element_type=jnp.float32,
    )


def row_max(scores):
    return jnp.max(scores, axis=1, keepdims=True)


def row_sum(scores):
    return jnp.sum(scores, axis=1, keepdims=True)


def band_kernel(
    meta_ref, slopes_ref, query_ref, keys_hbm, values_hbm, before_hbm, after_hbm,
    acc_ref, stat_ref,
    keys_ref, values_ref, gap_ref, max_ref, sum_ref, sems, *, blk_dev, total_blocks,
):
    head = pl.program_id(0)
    local = pl.program_id(1)
    margin = BAND * BT
    tok_rows = blk_dev * BT

    @pl.when(local == 0)
    def _():
        column = pl.ds(pl.multiple_of(head * DH, DH), DH)
        copies = []
        for which, (ref, whole) in enumerate(((keys_ref, keys_hbm), (values_ref, values_hbm))):
            copies += [
                pltpu.make_async_copy(
                    before_hbm.at[which, :, column], ref.at[pl.ds(0, margin)], sems.at[which, 0]
                ),
                pltpu.make_async_copy(
                    whole.at[:, column], ref.at[pl.ds(margin, tok_rows)], sems.at[which, 1]
                ),
                pltpu.make_async_copy(
                    after_hbm.at[which, :, column],
                    ref.at[pl.ds(margin + tok_rows, margin)],
                    sems.at[which, 2],
                ),
            ]
        for copy in copies:
            copy.start()
        gap_ref[...] = distances()
        for copy in copies:
            copy.wait()

    slope = slopes_ref[head] * LOG2E
    reach = meta_ref[local]
    block = meta_ref[blk_dev] * blk_dev + local
    query = query_ref[...]

    def rows_of(offset):
        return pl.ds(pl.multiple_of((local + BAND + offset) * BT, BT), BT)

    scores = pair_scores(query, keys_ref[rows_of(0), :], 0.0, slope, gap_ref[...])
    top = row_max(scores)
    weights = jnp.exp2(scores - top)
    max_ref[...] = top
    sum_ref[...] = row_sum(weights)
    acc_ref[...] = weighted(weights, values_ref[rows_of(0), :])

    for distance in range(1, BAND + 1):

        @pl.when(reach >= distance)
        def _():
            low = jnp.where(block >= distance, float(distance * BT), FAR_AWAY)
            high = jnp.where(block + distance < total_blocks, -float(distance * BT), -FAR_AWAY)
            gap = gap_ref[...]
            first = pair_scores(query, keys_ref[rows_of(-distance), :], low, slope, gap)
            second = pair_scores(query, keys_ref[rows_of(distance), :], high, slope, gap)
            old = max_ref[...]
            top = jnp.maximum(old, row_max(jnp.maximum(first, second)))
            shrink = jnp.exp2(old - top)
            first = jnp.exp2(first - top)
            second = jnp.exp2(second - top)
            max_ref[...] = top
            sum_ref[...] = sum_ref[...] * shrink + row_sum(first + second)
            acc_ref[...] = (
                acc_ref[...] * shrink
                + weighted(first, values_ref[rows_of(-distance), :])
                + weighted(second, values_ref[rows_of(distance), :])
            )

    total = sum_ref[...]
    acc_ref[...] = acc_ref[...] / total
    stat_ref[...] = jnp.broadcast_to(max_ref[...] + jnp.log2(total), (BT, DH))


def band_attention(meta, slopes, queries, key_rows, value_rows, before, after, total_blocks):
    tok_rows, channels = queries.shape
    blk_dev = tok_rows // BT
    heads = channels // DH
    any_spec = pl.BlockSpec(memory_space=pltpu.HBM)
    tile = pl.BlockSpec((BT, DH), lambda h, i, *_: (i, h))
    ext = tok_rows + 2 * BAND * BT
    return pl.pallas_call(
        functools.partial(band_kernel, blk_dev=blk_dev, total_blocks=total_blocks),
        out_shape=(
            jax.ShapeDtypeStruct((tok_rows, channels), jnp.float32),
            jax.ShapeDtypeStruct((tok_rows, channels), jnp.float32),
        ),
        grid_spec=pltpu.PrefetchScalarGridSpec(
            num_scalar_prefetch=2,
            grid=(heads, blk_dev),
            in_specs=[tile, any_spec, any_spec, any_spec, any_spec],
            out_specs=(tile, tile),
            scratch_shapes=[
                pltpu.VMEM((ext, DH), jnp.bfloat16),
                pltpu.VMEM((ext, DH), jnp.bfloat16),
                pltpu.VMEM((BT, BT), jnp.float32),
                pltpu.VMEM((BT, 1), jnp.float32),
                pltpu.VMEM((BT, 1), jnp.float32),
                pltpu.SemaphoreType.DMA((2, 3)),
            ],
        ),
        compiler_params=pltpu.CompilerParams(vmem_limit_bytes=24 * MIB),
        cost_estimate=pl.CostEstimate(
            flops=7 * 4 * tok_rows * BT * channels,
            transcendentals=7 * tok_rows * BT * heads,
            bytes_accessed=30 * MIB,
        ),
        name="band",
    )(meta, slopes, queries, key_rows, value_rows, before, after)


def gather_pieces(pieces, buffer_ref, sems, sources):
    if len(pieces) == 1:
        pieces = [pieces[0].at[s] for s in range(sources)]
    copies = [
        pltpu.make_async_copy(piece, buffer_ref.at[s], sems.at[s])
        for s, piece in enumerate(pieces)
    ]
    for copy in copies:
        copy.start()
    return copies


def place_of(slot, me, sources, split):
    source = lax.div(slot, CAP)
    if split:
        source = me - source
        source = jnp.where(source < 0, source + sources, source)
    return source, lax.rem(slot, CAP)


def far_kernel(
    meta_ref, slot_ref, block_ref, slopes_ref, query_ref, acc_ref, stat_ref, *refs, head, blk_dev,
    sources, group, split,
):
    if split:
        pieces = refs[:-5]
        weights_ref, out_ref, buffer_ref, gap_ref, sems = refs[-5:]
    else:
        pieces = refs[:-4]
        out_ref, buffer_ref, gap_ref, sems = refs[-4:]
    local = pl.program_id(0)

    @pl.when(local == 0)
    def _():
        copies = gather_pieces(pieces, buffer_ref, sems, sources)
        gap_ref[...] = distances()
        for copy in copies:
            copy.wait()

    slope = slopes_ref[head] * LOG2E
    me = meta_ref[blk_dev]
    gap = gap_ref[...]
    ones = jnp.ones((BT, DH), jnp.bfloat16)
    for part in range(group):
        i = local * group + part
        rows = pl.ds(part * BT, BT)
        block = me * blk_dev + i
        query = query_ref[rows, :]
        scores = []
        values = []
        for f in range(FAR):
            offset = ((block - block_ref[f, i]) * BT).astype(jnp.float32)
            source, rank = place_of(slot_ref[f, i], me, sources, split)
            key = buffer_ref[source, rank if split else rank * 2]
            scores.append(pair_scores(query, key, offset, slope, gap))
            if not split:
                values.append(jnp.concatenate([buffer_ref[source, rank * 2 + 1], ones], axis=1))
        band = stat_ref[rows, :]
        top = jnp.maximum(band[:, 0:1], row_max(jnp.maximum(scores[0], scores[1])))
        weights = [jnp.exp2(score - top) for score in scores]
        share = jnp.exp2(band - top)
        if split:
            scale = 1.0 / (share[:, 0:1] + row_sum(weights[0] + weights[1]))
            for f in range(FAR):
                weights_ref[rows, f * BT : (f + 1) * BT] = (weights[f] * scale).astype(jnp.bfloat16)
            out_ref[rows, :] = acc_ref[rows, :] * (share * scale)
        else:
            far = weighted(weights[0], values[0]) + weighted(weights[1], values[1])
            acc = acc_ref[rows, :] * share + far[:, :DH]
            out_ref[rows, :] = (acc / (share + far[:, DH:])).astype(jnp.bfloat16)


def far_attention(meta, slots, far_blocks, slopes, queries, acc, stat, pieces, head, sources):
    tok_rows = queries.shape[0]
    blk_dev = tok_rows // BT
    split = len(pieces) > 1
    group = 2 if blk_dev % 2 == 0 else 1
    tile = pl.BlockSpec((group * BT, DH), lambda i, *_: (i, head))
    hbm = pl.BlockSpec(memory_space=pltpu.HBM)
    out_shape = [jax.ShapeDtypeStruct((tok_rows, DH), jnp.float32 if split else jnp.bfloat16)]
    out_specs = [pl.BlockSpec((group * BT, DH), lambda i, *_: (i, 0))]
    if split:
        out_shape.insert(0, jax.ShapeDtypeStruct((tok_rows, FAR * BT), jnp.bfloat16))
        out_specs.insert(0, pl.BlockSpec((group * BT, FAR * BT), lambda i, *_: (i, 0)))
    return pl.pallas_call(
        functools.partial(
            far_kernel, head=head, blk_dev=blk_dev, sources=sources, group=group, split=split
        ),
        out_shape=out_shape,
        grid_spec=pltpu.PrefetchScalarGridSpec(
            num_scalar_prefetch=4,
            grid=(blk_dev // group,),
            in_specs=[tile, tile, tile] + [hbm] * len(pieces),
            out_specs=out_specs,
            scratch_shapes=[
                pltpu.VMEM((sources, CAP if split else CAP * 2, BT, DH), jnp.bfloat16),
                pltpu.VMEM((BT, BT), jnp.float32),
                pltpu.SemaphoreType.DMA((sources,)),
            ],
        ),
        compiler_params=pltpu.CompilerParams(vmem_limit_bytes=24 * MIB),
        cost_estimate=pl.CostEstimate(
            flops=2 * 4 * tok_rows * BT * DH,
            transcendentals=2 * tok_rows * BT,
            bytes_accessed=14 * MIB,
        ),
        name="far",
    )(meta, slots, far_blocks, slopes, queries, acc, stat, *pieces)


def value_kernel(me_ref, slot_ref, weights_ref, acc_ref, *refs, sources, group):
    pieces = refs[:-3]
    out_ref, buffer_ref, sems = refs[-3:]
    local = pl.program_id(0)

    @pl.when(local == 0)
    def _():
        for copy in gather_pieces(pieces, buffer_ref, sems, sources):
            copy.wait()

    for part in range(group):
        rows = pl.ds(part * BT, BT)
        acc = acc_ref[rows, :]
        for f in range(FAR):
            source, rank = place_of(slot_ref[f, local * group + part], me_ref[0], sources, True)
            acc = acc + weighted(
                weights_ref[rows, f * BT : (f + 1) * BT], buffer_ref[source, rank]
            )
        out_ref[rows, :] = acc.astype(jnp.bfloat16)


def far_values(me, slots, weights, acc, pieces, sources):
    tok_rows = acc.shape[0]
    blk_dev = tok_rows // BT
    group = 2 if blk_dev % 2 == 0 else 1
    hbm = pl.BlockSpec(memory_space=pltpu.HBM)
    return pl.pallas_call(
        functools.partial(value_kernel, sources=sources, group=group),
        out_shape=jax.ShapeDtypeStruct((tok_rows, DH), jnp.bfloat16),
        grid_spec=pltpu.PrefetchScalarGridSpec(
            num_scalar_prefetch=2,
            grid=(blk_dev // group,),
            in_specs=[
                pl.BlockSpec((group * BT, FAR * BT), lambda i, *_: (i, 0)),
                pl.BlockSpec((group * BT, DH), lambda i, *_: (i, 0)),
            ]
            + [hbm] * len(pieces),
            out_specs=pl.BlockSpec((group * BT, DH), lambda i, *_: (i, 0)),
            scratch_shapes=[
                pltpu.VMEM((sources, CAP, BT, DH), jnp.bfloat16),
                pltpu.SemaphoreType.DMA((sources,)),
            ],
        ),
        compiler_params=pltpu.CompilerParams(vmem_limit_bytes=16 * MIB),
        name="values",
    )(me, slots, weights, acc, *pieces)


def place_kernel(*refs, heads):
    parts = refs[:heads]
    out_ref, buffer_ref, in_sems, out_sems = refs[heads:]
    peers = parts[0].shape[0]
    width = heads * DH
    loads = [
        [
            pltpu.make_async_copy(
                part.at[g], buffer_ref.at[g, :, pl.ds(head * DH, DH)], in_sems.at[g, head]
            )
            for head, part in enumerate(parts)
        ]
        for g in range(peers)
    ]
    stores = [
        pltpu.make_async_copy(
            buffer_ref.at[g], out_ref.at[:, pl.ds(g * width, width)], out_sems.at[g]
        )
        for g in range(peers)
    ]
    for pair in loads:
        for load in pair:
            load.start()
    for pair, store in zip(loads, stores):
        for load in pair:
            load.wait()
        store.start()
    for store in stores:
        store.wait()


def place(parts):
    peers, rows, _ = parts[0].shape
    heads = len(parts)
    any_spec = pl.BlockSpec(memory_space=pl.ANY)
    return pl.pallas_call(
        functools.partial(place_kernel, heads=heads),
        out_shape=jax.ShapeDtypeStruct((rows, peers * heads * DH), parts[0].dtype),
        in_specs=[any_spec] * heads,
        out_specs=pl.BlockSpec(memory_space=pltpu.HBM),
        scratch_shapes=[
            pltpu.VMEM((peers, rows, heads * DH), parts[0].dtype),
            pltpu.SemaphoreType.DMA((peers, heads)),
            pltpu.SemaphoreType.DMA((peers,)),
        ],
        name="place",
    )(*parts)


def body(queries, key_rows, value_rows, band_reach, far_list, slopes):
    myself = lax.axis_index("seq")
    sources = lax.axis_size("seq")
    tok_rows, channels = key_rows.shape
    blk_dev = tok_rows // BT
    margin = BAND * BT
    heads = channels // DH
    up = [(i, i + 1) for i in range(sources - 1)]
    down = [(i + 1, i) for i in range(sources - 1)]

    table, slots = route(far_list, sources)
    asked = lax.all_to_all(table, "seq", split_axis=0, concat_axis=0, tiled=True)
    last = jnp.stack([key_rows[tok_rows - margin :], value_rows[tok_rows - margin :]])
    first = jnp.stack([key_rows[:margin], value_rows[:margin]])
    before = lax.ppermute(last, "seq", up)
    after = lax.ppermute(first, "seq", down)

    me = myself[None].astype(jnp.int32)
    keys_hbm, values_hbm = (
        pltpu.with_memory_space_constraint(x, pltpu.HBM) for x in (key_rows, value_rows)
    )
    incoming = []
    for head in range(heads):
        split = head == heads - 1
        outgoing = pack(asked, me, keys_hbm, values_hbm, head, split)
        if split:
            pieces = []
            for which in range(2):
                arrays = list(outgoing[which * sources : (which + 1) * sources])
                for shift in range(1, sources):
                    ring = [(i, (i + shift) % sources) for i in range(sources)]
                    arrays[shift] = lax.ppermute(arrays[shift], "seq", ring)
                pieces.append(arrays)
            incoming.append(pieces)
        else:
            incoming.append(
                [lax.all_to_all(outgoing[0], "seq", split_axis=0, concat_axis=0, tiled=True)]
            )

    meta = jnp.concatenate([band_reach, me])
    acc, stat = band_attention(
        meta, slopes, queries, key_rows, value_rows, before, after, blk_dev * sources
    )
    acc, stat, queries = (
        pltpu.with_memory_space_constraint(x, pltpu.HBM) for x in (acc, stat, queries)
    )
    parts = []
    for head in range(heads):
        split = head == heads - 1
        pieces = incoming[head][0] if split else incoming[head]
        attended = far_attention(
            meta, slots, far_list.T, slopes, queries, acc, stat, pieces, head, sources
        )
        if split:
            attended = far_values(me, slots, *attended, incoming[head][1], sources)
        else:
            attended = attended[0]
        parts.append(
            lax.all_to_all(
                attended.reshape(lax.axis_size("head"), -1, DH), "head",
                split_axis=0, concat_axis=0, tiled=True,
            )
        )
    return place(parts)


def solution(mesh):
    in_specs = (
        P("seq", "head"),
        P("seq", "head"),
        P("seq", "head"),
        P("seq"),
        P("seq", None),
        P("head"),
    )
    out_specs = P(("seq", "head"), None)

    return jax.shard_map(body, mesh=mesh, in_specs=in_specs, out_specs=out_specs, check_vma=False)
```

```python
import functools
import math

import jax
import jax.numpy as jnp
from jax import lax
from jax.experimental import pallas as pl
from jax.experimental.pallas import tpu as pltpu
from jax.sharding import PartitionSpec as P


BT = 256
BAND = 3
FAR = 2
CAP = 2
DH = 128
LOG2E = 1.4426950408889634
FAR_AWAY = 1e30
MIB = 1 << 20


def route_kernel(far_ref, table_ref, slot_ref, count_ref, *, sources, blk_dev):
    for s in range(sources):
        count_ref[s] = 0
        for r in range(CAP):
            table_ref[s, r] = 0

    def step(i, carry):
        for f in range(FAR):
            block = far_ref[f, i]
            s = lax.div(block, blk_dev)
            r = jnp.minimum(count_ref[s], CAP - 1)
            count_ref[s] = r + 1
            table_ref[s, r] = block - s * blk_dev
            slot_ref[f, i] = s * CAP + r
        return carry

    lax.fori_loop(0, blk_dev, step, 0)


def route(far_list, sources):
    blk_dev = far_list.shape[0]
    smem = pl.BlockSpec(memory_space=pltpu.SMEM)
    return pl.pallas_call(
        functools.partial(route_kernel, sources=sources, blk_dev=blk_dev),
        out_shape=(
            jax.ShapeDtypeStruct((sources, CAP), jnp.int32),
            jax.ShapeDtypeStruct((FAR, blk_dev), jnp.int32),
        ),
        in_specs=[smem],
        out_specs=(smem, smem),
        scratch_shapes=[pltpu.SMEM((sources,), jnp.int32)],
        name="route",
    )(far_list.T)


def pack_kernel(asked_ref, me_ref, keys_ref, values_ref, *refs, shifts):
    out_refs, sems = refs[:-1], refs[-1]
    copies = []
    for which, ref in enumerate((keys_ref, values_ref)):
        for shift in range(shifts):
            target = me_ref[0] + shift
            target = jnp.where(target >= shifts, target - shifts, target)
            for r in range(CAP):
                rows = pl.ds(pl.multiple_of(asked_ref[target, r] * BT, BT), BT)
                slot = r * 2 + which
                if len(out_refs) == 1:
                    dst = out_refs[0].at[target, slot]
                else:
                    dst = out_refs[which * shifts + shift].at[r]
                copy = pltpu.make_async_copy(ref.at[rows, :], dst, sems.at[shift, slot])
                copy.start()
                copies.append(copy)
    for copy in copies:
        copy.wait()


def pack(asked, me, key_rows, value_rows, head, split):
    shifts = asked.shape[0]
    tok_rows = key_rows.shape[0]
    hbm = pl.BlockSpec(memory_space=pltpu.HBM)
    column = pl.BlockSpec((tok_rows, DH), lambda i, *_: (0, head))
    if split:
        out_shape = (pltpu.HBM((CAP, BT, DH), key_rows.dtype),) * (2 * shifts)
    else:
        out_shape = (pltpu.HBM((shifts, CAP * 2, BT, DH), key_rows.dtype),)
    return pl.pallas_call(
        functools.partial(pack_kernel, shifts=shifts),
        out_shape=out_shape,
        grid_spec=pltpu.PrefetchScalarGridSpec(
            num_scalar_prefetch=2,
            grid=(1,),
            in_specs=[column, column],
            out_specs=(hbm,) * len(out_shape),
            scratch_shapes=[pltpu.SemaphoreType.DMA((shifts, CAP * 2))],
        ),
        compiler_params=pltpu.CompilerParams(vmem_limit_bytes=16 * MIB),
        name="pack",
    )(asked, me, key_rows, value_rows)


def distances():
    rows = lax.broadcasted_iota(jnp.int32, (BT, BT), 0)
    columns = lax.broadcasted_iota(jnp.int32, (BT, BT), 1)
    return (rows - columns).astype(jnp.float32)


def pair_scores(query, key, offset, slope, gap):
    product = lax.dot_general(
        query, key, (((1,), (1,)), ((), ())), preferred_element_type=jnp.float32
    )
    return product * (LOG2E / math.sqrt(DH)) - slope * jnp.abs(gap + offset)


def weighted(weights, value):
    return lax.dot_general(
        weights.astype(jnp.bfloat16), value, (((1,), (0,)), ((), ())),
        preferred_element_type=jnp.float32,
    )


def row_max(scores):
    return jnp.max(scores, axis=1, keepdims=True)


def row_sum(scores):
    return jnp.sum(scores, axis=1, keepdims=True)


def band_kernel(
    meta_ref, slopes_ref, query_ref, keys_hbm, values_hbm, *refs, blk_dev, total_blocks,
):
    before_hbm, after_hbm = refs[0:2], refs[2:4]
    acc_ref, stat_ref, keys_ref, values_ref, gap_ref, max_ref, sum_ref, sems = refs[4:]
    head = pl.program_id(0)
    local = pl.program_id(1)
    margin = BAND * BT
    tok_rows = blk_dev * BT

    @pl.when(local == 0)
    def _():
        column = pl.ds(pl.multiple_of(head * DH, DH), DH)
        copies = []
        for which, (ref, whole) in enumerate(((keys_ref, keys_hbm), (values_ref, values_hbm))):
            copies += [
                pltpu.make_async_copy(
                    before_hbm[which].at[:, column], ref.at[pl.ds(0, margin)], sems.at[which, 0]
                ),
                pltpu.make_async_copy(
                    whole.at[:, column], ref.at[pl.ds(margin, tok_rows)], sems.at[which, 1]
                ),
                pltpu.make_async_copy(
                    after_hbm[which].at[:, column],
                    ref.at[pl.ds(margin + tok_rows, margin)],
                    sems.at[which, 2],
                ),
            ]
        for copy in copies:
            copy.start()
        gap_ref[...] = distances()
        for copy in copies:
            copy.wait()

    slope = slopes_ref[head] * LOG2E
    reach = meta_ref[local]
    block = meta_ref[blk_dev] * blk_dev + local
    query = query_ref[...]

    def rows_of(offset):
        return pl.ds(pl.multiple_of((local + BAND + offset) * BT, BT), BT)

    scores = pair_scores(query, keys_ref[rows_of(0), :], 0.0, slope, gap_ref[...])
    top = row_max(scores)
    weights = jnp.exp2(scores - top)
    max_ref[...] = top
    sum_ref[...] = row_sum(weights)
    acc_ref[...] = weighted(weights, values_ref[rows_of(0), :])

    for distance in range(1, BAND + 1):

        @pl.when(reach >= distance)
        def _():
            low = jnp.where(block >= distance, float(distance * BT), FAR_AWAY)
            high = jnp.where(block + distance < total_blocks, -float(distance * BT), -FAR_AWAY)
            gap = gap_ref[...]
            first = pair_scores(query, keys_ref[rows_of(-distance), :], low, slope, gap)
            second = pair_scores(query, keys_ref[rows_of(distance), :], high, slope, gap)
            old = max_ref[...]
            top = jnp.maximum(old, row_max(jnp.maximum(first, second)))
            shrink = jnp.exp2(old - top)
            first = jnp.exp2(first - top)
            second = jnp.exp2(second - top)
            max_ref[...] = top
            sum_ref[...] = sum_ref[...] * shrink + row_sum(first + second)
            acc_ref[...] = (
                acc_ref[...] * shrink
                + weighted(first, values_ref[rows_of(-distance), :])
                + weighted(second, values_ref[rows_of(distance), :])
            )

    total = sum_ref[...]
    acc_ref[...] = acc_ref[...] / total
    stat_ref[...] = jnp.broadcast_to(max_ref[...] + jnp.log2(total), (BT, DH))


def band_attention(meta, slopes, queries, key_rows, value_rows, before, after, total_blocks):
    tok_rows, channels = queries.shape
    blk_dev = tok_rows // BT
    heads = channels // DH
    any_spec = pl.BlockSpec(memory_space=pltpu.HBM)
    tile = pl.BlockSpec((BT, DH), lambda h, i, *_: (i, h))
    ext = tok_rows + 2 * BAND * BT
    return pl.pallas_call(
        functools.partial(band_kernel, blk_dev=blk_dev, total_blocks=total_blocks),
        out_shape=(
            jax.ShapeDtypeStruct((tok_rows, channels), jnp.float32),
            jax.ShapeDtypeStruct((tok_rows, channels), jnp.float32),
        ),
        grid_spec=pltpu.PrefetchScalarGridSpec(
            num_scalar_prefetch=2,
            grid=(heads, blk_dev),
            in_specs=[tile] + [any_spec] * 6,
            out_specs=(tile, tile),
            scratch_shapes=[
                pltpu.VMEM((ext, DH), jnp.bfloat16),
                pltpu.VMEM((ext, DH), jnp.bfloat16),
                pltpu.VMEM((BT, BT), jnp.float32),
                pltpu.VMEM((BT, 1), jnp.float32),
                pltpu.VMEM((BT, 1), jnp.float32),
                pltpu.SemaphoreType.DMA((2, 3)),
            ],
        ),
        compiler_params=pltpu.CompilerParams(vmem_limit_bytes=24 * MIB),
        cost_estimate=pl.CostEstimate(
            flops=7 * 4 * tok_rows * BT * channels,
            transcendentals=7 * tok_rows * BT * heads,
            bytes_accessed=30 * MIB,
        ),
        name="band",
    )(meta, slopes, queries, key_rows, value_rows, *before, *after)


def gather_pieces(pieces, buffer_ref, sems, sources):
    if len(pieces) == 1:
        pieces = [pieces[0].at[s] for s in range(sources)]
    copies = [
        pltpu.make_async_copy(piece, buffer_ref.at[s], sems.at[s])
        for s, piece in enumerate(pieces)
    ]
    for copy in copies:
        copy.start()
    return copies


def place_of(slot, me, sources, split):
    source = lax.div(slot, CAP)
    if split:
        source = me - source
        source = jnp.where(source < 0, source + sources, source)
    return source, lax.rem(slot, CAP)


def far_kernel(
    meta_ref, slot_ref, block_ref, slopes_ref, query_ref, acc_ref, stat_ref, *refs, head, blk_dev,
    sources, group, split,
):
    if split:
        pieces = refs[:-5]
        weights_ref, out_ref, buffer_ref, gap_ref, sems = refs[-5:]
    else:
        pieces = refs[:-4]
        out_ref, buffer_ref, gap_ref, sems = refs[-4:]
    local = pl.program_id(0)

    @pl.when(local == 0)
    def _():
        copies = gather_pieces(pieces, buffer_ref, sems, sources)
        gap_ref[...] = distances()
        for copy in copies:
            copy.wait()

    slope = slopes_ref[head] * LOG2E
    me = meta_ref[blk_dev]
    gap = gap_ref[...]
    ones = jnp.ones((BT, DH), jnp.bfloat16)
    for part in range(group):
        i = local * group + part
        rows = pl.ds(part * BT, BT)
        block = me * blk_dev + i
        query = query_ref[rows, :]
        scores = []
        values = []
        for f in range(FAR):
            offset = ((block - block_ref[f, i]) * BT).astype(jnp.float32)
            source, rank = place_of(slot_ref[f, i], me, sources, split)
            key = buffer_ref[source, rank if split else rank * 2]
            scores.append(pair_scores(query, key, offset, slope, gap))
            if not split:
                values.append(jnp.concatenate([buffer_ref[source, rank * 2 + 1], ones], axis=1))
        band = stat_ref[rows, :]
        top = jnp.maximum(band[:, 0:1], row_max(jnp.maximum(scores[0], scores[1])))
        weights = [jnp.exp2(score - top) for score in scores]
        share = jnp.exp2(band - top)
        if split:
            scale = 1.0 / (share[:, 0:1] + row_sum(weights[0] + weights[1]))
            for f in range(FAR):
                weights_ref[rows, f * BT : (f + 1) * BT] = (weights[f] * scale).astype(jnp.bfloat16)
            out_ref[rows, :] = acc_ref[rows, :] * (share * scale)
        else:
            far = weighted(weights[0], values[0]) + weighted(weights[1], values[1])
            acc = acc_ref[rows, :] * share + far[:, :DH]
            out_ref[rows, :] = (acc / (share + far[:, DH:])).astype(jnp.bfloat16)


def far_attention(meta, slots, far_blocks, slopes, queries, acc, stat, pieces, head, sources):
    tok_rows = queries.shape[0]
    blk_dev = tok_rows // BT
    split = len(pieces) > 1
    group = 2 if blk_dev % 2 == 0 else 1
    tile = pl.BlockSpec((group * BT, DH), lambda i, *_: (i, head))
    hbm = pl.BlockSpec(memory_space=pltpu.HBM)
    out_shape = [jax.ShapeDtypeStruct((tok_rows, DH), jnp.float32 if split else jnp.bfloat16)]
    out_specs = [pl.BlockSpec((group * BT, DH), lambda i, *_: (i, 0))]
    if split:
        out_shape.insert(0, jax.ShapeDtypeStruct((tok_rows, FAR * BT), jnp.bfloat16))
        out_specs.insert(0, pl.BlockSpec((group * BT, FAR * BT), lambda i, *_: (i, 0)))
    return pl.pallas_call(
        functools.partial(
            far_kernel, head=head, blk_dev=blk_dev, sources=sources, group=group, split=split
        ),
        out_shape=out_shape,
        grid_spec=pltpu.PrefetchScalarGridSpec(
            num_scalar_prefetch=4,
            grid=(blk_dev // group,),
            in_specs=[tile, tile, tile] + [hbm] * len(pieces),
            out_specs=out_specs,
            scratch_shapes=[
                pltpu.VMEM((sources, CAP if split else CAP * 2, BT, DH), jnp.bfloat16),
                pltpu.VMEM((BT, BT), jnp.float32),
                pltpu.SemaphoreType.DMA((sources,)),
            ],
        ),
        compiler_params=pltpu.CompilerParams(vmem_limit_bytes=24 * MIB),
        cost_estimate=pl.CostEstimate(
            flops=2 * 4 * tok_rows * BT * DH,
            transcendentals=2 * tok_rows * BT,
            bytes_accessed=14 * MIB,
        ),
        name="far",
    )(meta, slots, far_blocks, slopes, queries, acc, stat, *pieces)


def value_kernel(me_ref, slot_ref, weights_hbm, acc_hbm, *refs, sources, blk_dev):
    pieces = refs[:-7]
    out_ref, weights_ref, acc_ref, buffer_ref, sems, weight_sems, acc_sems = refs[-7:]
    copies = gather_pieces(pieces, buffer_ref, sems, sources)
    rows = [pl.ds(i * BT, BT) for i in range(blk_dev)]
    weight_copies = [
        pltpu.make_async_copy(weights_hbm.at[r], weights_ref.at[r], weight_sems.at[i])
        for i, r in enumerate(rows)
    ]
    acc_copies = [
        pltpu.make_async_copy(acc_hbm.at[r], acc_ref.at[r], acc_sems.at[i])
        for i, r in enumerate(rows)
    ]
    for weight_copy, acc_copy in zip(weight_copies, acc_copies):
        weight_copy.start()
        acc_copy.start()
    for copy in copies:
        copy.wait()
    for i, r in enumerate(rows):
        weight_copies[i].wait()
        acc_copies[i].wait()
        acc = acc_ref[r, :]
        for f in range(FAR):
            source, rank = place_of(slot_ref[f, i], me_ref[0], sources, True)
            acc = acc + weighted(weights_ref[r, f * BT : (f + 1) * BT], buffer_ref[source, rank])
        out_ref[r, :] = acc.astype(jnp.bfloat16)


def far_values(me, slots, weights, acc, pieces, sources):
    tok_rows = acc.shape[0]
    blk_dev = tok_rows // BT
    any_spec = pl.BlockSpec(memory_space=pl.ANY)
    return pl.pallas_call(
        functools.partial(value_kernel, sources=sources, blk_dev=blk_dev),
        out_shape=jax.ShapeDtypeStruct((tok_rows, DH), jnp.bfloat16),
        grid_spec=pltpu.PrefetchScalarGridSpec(
            num_scalar_prefetch=2,
            grid=(1,),
            in_specs=[any_spec] * (2 + len(pieces)),
            out_specs=pl.BlockSpec((tok_rows, DH), lambda i, *_: (0, 0)),
            scratch_shapes=[
                pltpu.VMEM(weights.shape, weights.dtype),
                pltpu.VMEM(acc.shape, acc.dtype),
                pltpu.VMEM((sources, CAP, BT, DH), jnp.bfloat16),
                pltpu.SemaphoreType.DMA((sources,)),
                pltpu.SemaphoreType.DMA((blk_dev,)),
                pltpu.SemaphoreType.DMA((blk_dev,)),
            ],
        ),
        compiler_params=pltpu.CompilerParams(vmem_limit_bytes=20 * MIB),
        name="values",
    )(me, slots, weights, acc, *pieces)


def place_kernel(*refs, heads):
    parts = refs[:heads]
    out_ref, buffer_ref, in_sems, out_sems = refs[heads:]
    peers = parts[0].shape[0]
    width = heads * DH
    loads = [
        [
            pltpu.make_async_copy(
                part.at[g], buffer_ref.at[g, :, pl.ds(head * DH, DH)], in_sems.at[g, head]
            )
            for head, part in enumerate(parts)
        ]
        for g in range(peers)
    ]
    stores = [
        pltpu.make_async_copy(
            buffer_ref.at[g], out_ref.at[:, pl.ds(g * width, width)], out_sems.at[g]
        )
        for g in range(peers)
    ]
    for pair in loads:
        for load in pair:
            load.start()
    for pair, store in zip(loads, stores):
        for load in pair:
            load.wait()
        store.start()
    for store in stores:
        store.wait()


def place(parts):
    peers, rows, _ = parts[0].shape
    heads = len(parts)
    any_spec = pl.BlockSpec(memory_space=pl.ANY)
    return pl.pallas_call(
        functools.partial(place_kernel, heads=heads),
        out_shape=jax.ShapeDtypeStruct((rows, peers * heads * DH), parts[0].dtype),
        in_specs=[any_spec] * heads,
        out_specs=pl.BlockSpec(memory_space=pltpu.HBM),
        scratch_shapes=[
            pltpu.VMEM((peers, rows, heads * DH), parts[0].dtype),
            pltpu.SemaphoreType.DMA((peers, heads)),
            pltpu.SemaphoreType.DMA((peers,)),
        ],
        name="place",
    )(*parts)


def body(queries, key_rows, value_rows, band_reach, far_list, slopes):
    myself = lax.axis_index("seq")
    sources = lax.axis_size("seq")
    tok_rows, channels = key_rows.shape
    blk_dev = tok_rows // BT
    margin = BAND * BT
    heads = channels // DH
    up = [(i, i + 1) for i in range(sources - 1)]
    down = [(i + 1, i) for i in range(sources - 1)]

    before, after = [], []
    for rows in (key_rows, value_rows):
        before.append(lax.ppermute(rows[tok_rows - margin :], "seq", up))
        after.append(lax.ppermute(rows[:margin], "seq", down))
    table, slots = route(far_list, sources)
    asked = lax.all_to_all(table, "seq", split_axis=0, concat_axis=0, tiled=True)
    me = myself[None].astype(jnp.int32)
    keys_hbm, values_hbm = (
        pltpu.with_memory_space_constraint(x, pltpu.HBM) for x in (key_rows, value_rows)
    )
    incoming = []
    for head in range(heads):
        split = head == heads - 1
        outgoing = pack(asked, me, keys_hbm, values_hbm, head, split)
        if split:
            pieces = []
            for which in range(2):
                arrays = list(outgoing[which * sources : (which + 1) * sources])
                for shift in range(1, sources):
                    ring = [(i, (i + shift) % sources) for i in range(sources)]
                    arrays[shift] = lax.ppermute(arrays[shift], "seq", ring)
                pieces.append([pltpu.with_memory_space_constraint(x, pltpu.HBM) for x in arrays])
            incoming.append(pieces)
        else:
            incoming.append(
                [lax.all_to_all(outgoing[0], "seq", split_axis=0, concat_axis=0, tiled=True)]
            )

    meta = jnp.concatenate([band_reach, me])
    acc, stat = band_attention(
        meta, slopes, queries, key_rows, value_rows, before, after, blk_dev * sources
    )
    acc, stat, queries = (
        pltpu.with_memory_space_constraint(x, pltpu.HBM) for x in (acc, stat, queries)
    )
    parts = []
    for head in range(heads):
        split = head == heads - 1
        pieces = incoming[head][0] if split else incoming[head]
        attended = far_attention(
            meta, slots, far_list.T, slopes, queries, acc, stat, pieces, head, sources
        )
        if split:
            attended = far_values(me, slots, *attended, incoming[head][1], sources)
        else:
            attended = attended[0]
        parts.append(
            lax.all_to_all(
                attended.reshape(lax.axis_size("head"), -1, DH), "head",
                split_axis=0, concat_axis=0, tiled=True,
            )
        )
    return place(parts)


def solution(mesh):
    in_specs = (
        P("seq", "head"),
        P("seq", "head"),
        P("seq", "head"),
        P("seq"),
        P("seq", None),
        P("head"),
    )
    out_specs = P(("seq", "head"), None)

    return jax.shard_map(body, mesh=mesh, in_specs=in_specs, out_specs=out_specs, check_vma=False)
```

```python
import functools
import math

import jax
import jax.numpy as jnp
from jax import lax
from jax.experimental import pallas as pl
from jax.experimental.pallas import tpu as pltpu
from jax.sharding import PartitionSpec as P


BT = 256
BAND = 3
FAR = 2
CAP = 2
DH = 128
LOG2E = 1.4426950408889634
FAR_AWAY = 1e30
MIB = 1 << 20


def route_kernel(far_ref, table_ref, slot_ref, count_ref, *, sources, blk_dev):
    for s in range(sources):
        count_ref[s] = 0
        for r in range(CAP):
            table_ref[s, r] = 0

    def step(i, carry):
        for f in range(FAR):
            block = far_ref[f, i]
            s = lax.div(block, blk_dev)
            r = jnp.minimum(count_ref[s], CAP - 1)
            count_ref[s] = r + 1
            table_ref[s, r] = block - s * blk_dev
            slot_ref[f, i] = s * CAP + r
        return carry

    lax.fori_loop(0, blk_dev, step, 0)


def route(far_list, sources):
    blk_dev = far_list.shape[0]
    smem = pl.BlockSpec(memory_space=pltpu.SMEM)
    return pl.pallas_call(
        functools.partial(route_kernel, sources=sources, blk_dev=blk_dev),
        out_shape=(
            jax.ShapeDtypeStruct((sources, CAP), jnp.int32),
            jax.ShapeDtypeStruct((FAR, blk_dev), jnp.int32),
        ),
        in_specs=[smem],
        out_specs=(smem, smem),
        scratch_shapes=[pltpu.SMEM((sources,), jnp.int32)],
        name="route",
    )(far_list.T)


def pack_kernel(asked_ref, me_ref, keys_ref, values_ref, *refs, shifts):
    out_refs, sems = refs[:-1], refs[-1]
    copies = []
    for which, ref in enumerate((keys_ref, values_ref)):
        for shift in range(shifts):
            target = me_ref[0] + shift
            target = jnp.where(target >= shifts, target - shifts, target)
            for r in range(CAP):
                rows = pl.ds(pl.multiple_of(asked_ref[target, r] * BT, BT), BT)
                slot = r * 2 + which
                if len(out_refs) == 1:
                    dst = out_refs[0].at[target, slot]
                else:
                    dst = out_refs[which * shifts + shift].at[r]
                copy = pltpu.make_async_copy(ref.at[rows, :], dst, sems.at[shift, slot])
                copy.start()
                copies.append(copy)
    for copy in copies:
        copy.wait()


def pack(asked, me, key_rows, value_rows, head, split):
    shifts = asked.shape[0]
    tok_rows = key_rows.shape[0]
    hbm = pl.BlockSpec(memory_space=pltpu.HBM)
    column = pl.BlockSpec((tok_rows, DH), lambda i, *_: (0, head))
    if split:
        out_shape = (pltpu.HBM((CAP, BT, DH), key_rows.dtype),) * (2 * shifts)
    else:
        out_shape = (pltpu.HBM((shifts, CAP * 2, BT, DH), key_rows.dtype),)
    return pl.pallas_call(
        functools.partial(pack_kernel, shifts=shifts),
        out_shape=out_shape,
        grid_spec=pltpu.PrefetchScalarGridSpec(
            num_scalar_prefetch=2,
            grid=(1,),
            in_specs=[column, column],
            out_specs=(hbm,) * len(out_shape),
            scratch_shapes=[pltpu.SemaphoreType.DMA((shifts, CAP * 2))],
        ),
        compiler_params=pltpu.CompilerParams(vmem_limit_bytes=16 * MIB),
        name="pack",
    )(asked, me, key_rows, value_rows)


def distances():
    rows = lax.broadcasted_iota(jnp.int32, (BT, BT), 0)
    columns = lax.broadcasted_iota(jnp.int32, (BT, BT), 1)
    return (rows - columns).astype(jnp.float32)


def pair_scores(query, key, offset, slope, gap):
    product = lax.dot_general(
        query, key, (((1,), (1,)), ((), ())), preferred_element_type=jnp.float32
    )
    return product * (LOG2E / math.sqrt(DH)) - slope * jnp.abs(gap + offset)


def weighted(weights, value):
    return lax.dot_general(
        weights.astype(jnp.bfloat16), value, (((1,), (0,)), ((), ())),
        preferred_element_type=jnp.float32,
    )


def row_max(scores):
    return jnp.max(scores, axis=1, keepdims=True)


def row_sum(scores):
    return jnp.sum(scores, axis=1, keepdims=True)


def band_kernel(
    meta_ref, slopes_ref, query_ref, keys_hbm, values_hbm, before_hbm, after_hbm,
    acc_ref, stat_ref,
    keys_ref, values_ref, gap_ref, max_ref, sum_ref, sems, *, blk_dev, total_blocks,
):
    head = pl.program_id(0)
    local = pl.program_id(1)
    margin = BAND * BT
    tok_rows = blk_dev * BT

    @pl.when(local == 0)
    def _():
        column = pl.ds(pl.multiple_of(head * DH, DH), DH)
        copies = []
        for which, (ref, whole) in enumerate(((keys_ref, keys_hbm), (values_ref, values_hbm))):
            copies += [
                pltpu.make_async_copy(
                    before_hbm.at[which, :, column], ref.at[pl.ds(0, margin)], sems.at[which, 0]
                ),
                pltpu.make_async_copy(
                    whole.at[:, column], ref.at[pl.ds(margin, tok_rows)], sems.at[which, 1]
                ),
                pltpu.make_async_copy(
                    after_hbm.at[which, :, column],
                    ref.at[pl.ds(margin + tok_rows, margin)],
                    sems.at[which, 2],
                ),
            ]
        for copy in copies:
            copy.start()
        gap_ref[...] = distances()
        for copy in copies:
            copy.wait()

    slope = slopes_ref[head] * LOG2E
    reach = meta_ref[local]
    block = meta_ref[blk_dev] * blk_dev + local
    query = query_ref[...]

    def rows_of(offset):
        return pl.ds(pl.multiple_of((local + BAND + offset) * BT, BT), BT)

    scores = pair_scores(query, keys_ref[rows_of(0), :], 0.0, slope, gap_ref[...])
    top = row_max(scores)
    weights = jnp.exp2(scores - top)
    max_ref[...] = top
    sum_ref[...] = row_sum(weights)
    acc_ref[...] = weighted(weights, values_ref[rows_of(0), :])

    for distance in range(1, BAND + 1):

        @pl.when(reach >= distance)
        def _():
            low = jnp.where(block >= distance, float(distance * BT), FAR_AWAY)
            high = jnp.where(block + distance < total_blocks, -float(distance * BT), -FAR_AWAY)
            gap = gap_ref[...]
            first = pair_scores(query, keys_ref[rows_of(-distance), :], low, slope, gap)
            second = pair_scores(query, keys_ref[rows_of(distance), :], high, slope, gap)
            old = max_ref[...]
            top = jnp.maximum(old, row_max(jnp.maximum(first, second)))
            shrink = jnp.exp2(old - top)
            first = jnp.exp2(first - top)
            second = jnp.exp2(second - top)
            max_ref[...] = top
            sum_ref[...] = sum_ref[...] * shrink + row_sum(first + second)
            acc_ref[...] = (
                acc_ref[...] * shrink
                + weighted(first, values_ref[rows_of(-distance), :])
                + weighted(second, values_ref[rows_of(distance), :])
            )

    total = sum_ref[...]
    acc_ref[...] = acc_ref[...] / total
    stat_ref[...] = jnp.broadcast_to(max_ref[...] + jnp.log2(total), (BT, DH))


def band_attention(meta, slopes, queries, key_rows, value_rows, before, after, total_blocks):
    tok_rows, channels = queries.shape
    blk_dev = tok_rows // BT
    heads = channels // DH
    any_spec = pl.BlockSpec(memory_space=pltpu.HBM)
    tile = pl.BlockSpec((BT, DH), lambda h, i, *_: (i, h))
    ext = tok_rows + 2 * BAND * BT
    return pl.pallas_call(
        functools.partial(band_kernel, blk_dev=blk_dev, total_blocks=total_blocks),
        out_shape=(
            jax.ShapeDtypeStruct((tok_rows, channels), jnp.float32),
            jax.ShapeDtypeStruct((tok_rows, channels), jnp.float32),
        ),
        grid_spec=pltpu.PrefetchScalarGridSpec(
            num_scalar_prefetch=2,
            grid=(heads, blk_dev),
            in_specs=[tile, any_spec, any_spec, any_spec, any_spec],
            out_specs=(tile, tile),
            scratch_shapes=[
                pltpu.VMEM((ext, DH), jnp.bfloat16),
                pltpu.VMEM((ext, DH), jnp.bfloat16),
                pltpu.VMEM((BT, BT), jnp.float32),
                pltpu.VMEM((BT, 1), jnp.float32),
                pltpu.VMEM((BT, 1), jnp.float32),
                pltpu.SemaphoreType.DMA((2, 3)),
            ],
        ),
        compiler_params=pltpu.CompilerParams(vmem_limit_bytes=12 * MIB),
        cost_estimate=pl.CostEstimate(
            flops=7 * 4 * tok_rows * BT * channels,
            transcendentals=7 * tok_rows * BT * heads,
            bytes_accessed=30 * MIB,
        ),
        name="band",
    )(meta, slopes, queries, key_rows, value_rows, before, after)


def gather_pieces(pieces, buffer_ref, sems, sources):
    if len(pieces) == 1:
        pieces = [pieces[0].at[s] for s in range(sources)]
    copies = [
        pltpu.make_async_copy(piece, buffer_ref.at[s], sems.at[s])
        for s, piece in enumerate(pieces)
    ]
    for copy in copies:
        copy.start()
    return copies


def place_of(slot, me, sources, split):
    source = lax.div(slot, CAP)
    if split:
        source = me - source
        source = jnp.where(source < 0, source + sources, source)
    return source, lax.rem(slot, CAP)


def far_kernel(
    meta_ref, slot_ref, block_ref, slopes_ref, query_ref, acc_ref, stat_ref, *refs, head, blk_dev,
    sources, group, split,
):
    if split:
        pieces = refs[:-5]
        weights_ref, out_ref, buffer_ref, gap_ref, sems = refs[-5:]
    else:
        pieces = refs[:-4]
        out_ref, buffer_ref, gap_ref, sems = refs[-4:]
    local = pl.program_id(0)

    @pl.when(local == 0)
    def _():
        copies = gather_pieces(pieces, buffer_ref, sems, sources)
        gap_ref[...] = distances()
        for copy in copies:
            copy.wait()

    slope = slopes_ref[head] * LOG2E
    me = meta_ref[blk_dev]
    gap = gap_ref[...]
    ones = jnp.ones((BT, DH), jnp.bfloat16)
    for part in range(group):
        i = local * group + part
        rows = pl.ds(part * BT, BT)
        block = me * blk_dev + i
        query = query_ref[rows, :]
        scores = []
        values = []
        for f in range(FAR):
            offset = ((block - block_ref[f, i]) * BT).astype(jnp.float32)
            source, rank = place_of(slot_ref[f, i], me, sources, split)
            key = buffer_ref[source, rank if split else rank * 2]
            scores.append(pair_scores(query, key, offset, slope, gap))
            if not split:
                values.append(jnp.concatenate([buffer_ref[source, rank * 2 + 1], ones], axis=1))
        band = stat_ref[rows, :]
        top = jnp.maximum(band[:, 0:1], row_max(jnp.maximum(scores[0], scores[1])))
        weights = [jnp.exp2(score - top) for score in scores]
        share = jnp.exp2(band - top)
        if split:
            scale = 1.0 / (share[:, 0:1] + row_sum(weights[0] + weights[1]))
            for f in range(FAR):
                weights_ref[rows, f * BT : (f + 1) * BT] = (weights[f] * scale).astype(jnp.bfloat16)
            out_ref[rows, :] = acc_ref[rows, :] * (share * scale)
        else:
            far = weighted(weights[0], values[0]) + weighted(weights[1], values[1])
            acc = acc_ref[rows, :] * share + far[:, :DH]
            out_ref[rows, :] = (acc / (share + far[:, DH:])).astype(jnp.bfloat16)


def far_attention(meta, slots, far_blocks, slopes, queries, acc, stat, pieces, head, sources):
    tok_rows = queries.shape[0]
    blk_dev = tok_rows // BT
    split = len(pieces) > 1
    group = 2 if blk_dev % 2 == 0 else 1
    tile = pl.BlockSpec((group * BT, DH), lambda i, *_: (i, head))
    hbm = pl.BlockSpec(memory_space=pltpu.HBM)
    out_shape = [jax.ShapeDtypeStruct((tok_rows, DH), jnp.float32 if split else jnp.bfloat16)]
    out_specs = [pl.BlockSpec((group * BT, DH), lambda i, *_: (i, 0))]
    if split:
        out_shape = [
            pltpu.VMEM((tok_rows, FAR * BT), jnp.bfloat16),
            pltpu.VMEM((tok_rows, DH), jnp.float32),
        ]
        out_specs.insert(0, pl.BlockSpec((group * BT, FAR * BT), lambda i, *_: (i, 0)))
    return pl.pallas_call(
        functools.partial(
            far_kernel, head=head, blk_dev=blk_dev, sources=sources, group=group, split=split
        ),
        out_shape=out_shape,
        grid_spec=pltpu.PrefetchScalarGridSpec(
            num_scalar_prefetch=4,
            grid=(blk_dev // group,),
            in_specs=[tile, tile, tile] + [hbm] * len(pieces),
            out_specs=out_specs,
            scratch_shapes=[
                pltpu.VMEM((sources, CAP if split else CAP * 2, BT, DH), jnp.bfloat16),
                pltpu.VMEM((BT, BT), jnp.float32),
                pltpu.SemaphoreType.DMA((sources,)),
            ],
        ),
        compiler_params=pltpu.CompilerParams(vmem_limit_bytes=12 * MIB),
        cost_estimate=pl.CostEstimate(
            flops=2 * 4 * tok_rows * BT * DH,
            transcendentals=2 * tok_rows * BT,
            bytes_accessed=14 * MIB,
        ),
        name="far",
    )(meta, slots, far_blocks, slopes, queries, acc, stat, *pieces)


def value_kernel(me_ref, slot_ref, weights_ref, acc_ref, *refs, sources, blk_dev):
    pieces = refs[:-2]
    out_ref, buffer_ref = refs[-2:]
    for s, piece in enumerate(pieces):
        buffer_ref[s] = piece[...]
    for i in range(blk_dev):
        r = pl.ds(i * BT, BT)
        acc = acc_ref[r, :]
        for f in range(FAR):
            source, rank = place_of(slot_ref[f, i], me_ref[0], sources, True)
            acc = acc + weighted(weights_ref[r, f * BT : (f + 1) * BT], buffer_ref[source, rank])
        out_ref[r, :] = acc.astype(jnp.bfloat16)


def far_values(me, slots, weights, acc, pieces, sources):
    tok_rows = acc.shape[0]
    blk_dev = tok_rows // BT
    smem = pl.BlockSpec(memory_space=pltpu.SMEM)
    vmem = pl.BlockSpec(memory_space=pltpu.VMEM)
    return pl.pallas_call(
        functools.partial(value_kernel, sources=sources, blk_dev=blk_dev),
        out_shape=pltpu.VMEM((tok_rows, DH), jnp.bfloat16),
        in_specs=[smem, smem] + [vmem] * (2 + len(pieces)),
        out_specs=vmem,
        scratch_shapes=[pltpu.VMEM((sources, CAP, BT, DH), jnp.bfloat16)],
        compiler_params=pltpu.CompilerParams(vmem_limit_bytes=4 * MIB),
        name="values",
    )(me, slots, weights, acc, *pieces)


def place_kernel(*refs, heads):
    parts = refs[:heads]
    out_ref, sems = refs[heads:]
    peers = parts[0].shape[0]
    width = heads * DH
    copies = [
        pltpu.make_async_copy(
            part.at[g], out_ref.at[:, pl.ds(g * width + head * DH, DH)], sems.at[g, head]
        )
        for head, part in enumerate(parts)
        for g in range(peers)
    ]
    for copy in copies:
        copy.start()
    for copy in copies:
        copy.wait()


def place(parts):
    peers, rows, _ = parts[0].shape
    heads = len(parts)
    return pl.pallas_call(
        functools.partial(place_kernel, heads=heads),
        out_shape=jax.ShapeDtypeStruct((rows, peers * heads * DH), parts[0].dtype),
        in_specs=[pl.BlockSpec(memory_space=pltpu.VMEM)] * heads,
        out_specs=pl.BlockSpec(memory_space=pltpu.HBM),
        scratch_shapes=[pltpu.SemaphoreType.DMA((peers, heads))],
        name="place",
    )(*(pltpu.with_memory_space_constraint(part, pltpu.VMEM) for part in parts))


def body(queries, key_rows, value_rows, band_reach, far_list, slopes):
    myself = lax.axis_index("seq")
    sources = lax.axis_size("seq")
    tok_rows, channels = key_rows.shape
    blk_dev = tok_rows // BT
    margin = BAND * BT
    heads = channels // DH
    up = [(i, i + 1) for i in range(sources - 1)]
    down = [(i + 1, i) for i in range(sources - 1)]

    table, slots = route(far_list, sources)
    asked = lax.all_to_all(table, "seq", split_axis=0, concat_axis=0, tiled=True)
    last = jnp.stack([key_rows[tok_rows - margin :], value_rows[tok_rows - margin :]])
    first = jnp.stack([key_rows[:margin], value_rows[:margin]])
    before = lax.ppermute(last, "seq", up)
    after = lax.ppermute(first, "seq", down)

    me = myself[None].astype(jnp.int32)
    keys_hbm, values_hbm = (
        pltpu.with_memory_space_constraint(x, pltpu.HBM) for x in (key_rows, value_rows)
    )
    incoming = []
    for head in range(heads):
        split = head == heads - 1
        outgoing = pack(asked, me, keys_hbm, values_hbm, head, split)
        if split:
            pieces = []
            for which, kind in enumerate(("key", "value")):
                arrays = list(outgoing[which * sources : (which + 1) * sources])
                for shift in range(1, sources):
                    ring = [(i, (i + shift) % sources) for i in range(sources)]
                    arrays[shift] = lax.ppermute(arrays[shift], "seq", ring)
                space = pltpu.HBM if kind == "key" else pltpu.VMEM
                pieces.append([pltpu.with_memory_space_constraint(x, space) for x in arrays])
            incoming.append(pieces)
        else:
            incoming.append(
                [lax.all_to_all(outgoing[0], "seq", split_axis=0, concat_axis=0, tiled=True)]
            )

    meta = jnp.concatenate([band_reach, me])
    acc, stat = band_attention(
        meta, slopes, queries, key_rows, value_rows, before, after, blk_dev * sources
    )
    acc, stat, queries = (
        pltpu.with_memory_space_constraint(x, pltpu.HBM) for x in (acc, stat, queries)
    )
    parts = []
    for head in range(heads):
        split = head == heads - 1
        pieces = incoming[head][0] if split else incoming[head]
        attended = far_attention(
            meta, slots, far_list.T, slopes, queries, acc, stat, pieces, head, sources
        )
        if split:
            attended = far_values(me, slots, *attended, incoming[head][1], sources)
        else:
            attended = attended[0]
        parts.append(
            lax.all_to_all(
                attended.reshape(lax.axis_size("head"), -1, DH), "head",
                split_axis=0, concat_axis=0, tiled=True,
            )
        )
    return place(parts)


def solution(mesh):
    in_specs = (
        P("seq", "head"),
        P("seq", "head"),
        P("seq", "head"),
        P("seq"),
        P("seq", None),
        P("head"),
    )
    out_specs = P(("seq", "head"), None)

    return jax.shard_map(body, mesh=mesh, in_specs=in_specs, out_specs=out_specs, check_vma=False)
```

```python
import functools
import math

import jax
import jax.numpy as jnp
from jax import lax
from jax.experimental import pallas as pl
from jax.experimental.pallas import tpu as pltpu
from jax.sharding import PartitionSpec as P


BT = 256
BAND = 3
FAR = 2
CAP = 2
DH = 128
LOG2E = 1.4426950408889634
FAR_AWAY = 1e30
MIB = 1 << 20


def route_kernel(far_ref, table_ref, slot_ref, count_ref, *, sources, blk_dev):
    for s in range(sources):
        count_ref[s] = 0
        for r in range(CAP):
            table_ref[s, r] = 0

    def step(i, carry):
        for f in range(FAR):
            block = far_ref[f, i]
            s = lax.div(block, blk_dev)
            r = jnp.minimum(count_ref[s], CAP - 1)
            count_ref[s] = r + 1
            table_ref[s, r] = block - s * blk_dev
            slot_ref[f, i] = s * CAP + r
        return carry

    lax.fori_loop(0, blk_dev, step, 0)


def route(far_list, sources):
    blk_dev = far_list.shape[0]
    smem = pl.BlockSpec(memory_space=pltpu.SMEM)
    return pl.pallas_call(
        functools.partial(route_kernel, sources=sources, blk_dev=blk_dev),
        out_shape=(
            jax.ShapeDtypeStruct((sources, CAP), jnp.int32),
            jax.ShapeDtypeStruct((FAR, blk_dev), jnp.int32),
        ),
        in_specs=[smem],
        out_specs=(smem, smem),
        scratch_shapes=[pltpu.SMEM((sources,), jnp.int32)],
        name="route",
    )(far_list.T)


def pack_kernel(asked_ref, me_ref, keys_ref, values_ref, *refs, shifts):
    out_refs, sems = refs[:-1], refs[-1]
    copies = []
    for which, ref in enumerate((keys_ref, values_ref)):
        for shift in range(shifts):
            target = me_ref[0] + shift
            target = jnp.where(target >= shifts, target - shifts, target)
            for r in range(CAP):
                rows = pl.ds(pl.multiple_of(asked_ref[target, r] * BT, BT), BT)
                slot = r * 2 + which
                if len(out_refs) == 1:
                    dst = out_refs[0].at[target, slot]
                else:
                    dst = out_refs[which * shifts + shift].at[r]
                copy = pltpu.make_async_copy(ref.at[rows, :], dst, sems.at[shift, slot])
                copy.start()
                copies.append(copy)
    for copy in copies:
        copy.wait()


def pack(asked, me, key_rows, value_rows, head, split):
    shifts = asked.shape[0]
    tok_rows = key_rows.shape[0]
    hbm = pl.BlockSpec(memory_space=pltpu.HBM)
    column = pl.BlockSpec((tok_rows, DH), lambda i, *_: (0, head))
    if split:
        out_shape = (pltpu.HBM((CAP, BT, DH), key_rows.dtype),) * (2 * shifts)
    else:
        out_shape = (pltpu.HBM((shifts, CAP * 2, BT, DH), key_rows.dtype),)
    return pl.pallas_call(
        functools.partial(pack_kernel, shifts=shifts),
        out_shape=out_shape,
        grid_spec=pltpu.PrefetchScalarGridSpec(
            num_scalar_prefetch=2,
            grid=(1,),
            in_specs=[column, column],
            out_specs=(hbm,) * len(out_shape),
            scratch_shapes=[pltpu.SemaphoreType.DMA((shifts, CAP * 2))],
        ),
        compiler_params=pltpu.CompilerParams(vmem_limit_bytes=16 * MIB),
        name="pack",
    )(asked, me, key_rows, value_rows)


def fill_bias(bias_ref, slope):
    rows = lax.broadcasted_iota(jnp.int32, (BT, BT), 0)
    columns = lax.broadcasted_iota(jnp.int32, (BT, BT), 1)
    gap = (rows - columns).astype(jnp.float32) * slope
    bias_ref[0] = gap
    bias_ref[1] = -gap
    bias_ref[2] = jnp.abs(gap)


def pair_scores(query, key, bias):
    product = lax.dot_general(
        query, key, (((1,), (1,)), ((), ())), preferred_element_type=jnp.float32
    )
    return product * (LOG2E / math.sqrt(DH)) - bias


def weighted(weights, value):
    return lax.dot_general(
        weights.astype(jnp.bfloat16), value, (((1,), (0,)), ((), ())),
        preferred_element_type=jnp.float32,
    )


def row_max(scores):
    return jnp.max(scores, axis=1, keepdims=True)


def band_kernel(
    meta_ref, slopes_ref, query_ref, keys_hbm, values_hbm, before_hbm, after_hbm,
    acc_ref, stat_ref,
    keys_ref, values_ref, bias_ref, max_ref, acc_ref2, sems, *, blk_dev, total_blocks,
):
    head = pl.program_id(0)
    local = pl.program_id(1)
    margin = BAND * BT
    tok_rows = blk_dev * BT
    slope = slopes_ref[head] * LOG2E

    @pl.when(local == 0)
    def _():
        column = pl.ds(pl.multiple_of(head * DH, DH), DH)
        copies = []
        for which, (ref, whole) in enumerate(((keys_ref, keys_hbm), (values_ref, values_hbm))):
            copies += [
                pltpu.make_async_copy(
                    before_hbm.at[which, :, column], ref.at[pl.ds(0, margin)], sems.at[which, 0]
                ),
                pltpu.make_async_copy(
                    whole.at[:, column], ref.at[pl.ds(margin, tok_rows)], sems.at[which, 1]
                ),
                pltpu.make_async_copy(
                    after_hbm.at[which, :, column],
                    ref.at[pl.ds(margin + tok_rows, margin)],
                    sems.at[which, 2],
                ),
            ]
        for copy in copies:
            copy.start()
        fill_bias(bias_ref, slope)
        for copy in copies:
            copy.wait()

    reach = meta_ref[local]
    block = meta_ref[blk_dev] * blk_dev + local
    query = query_ref[...]
    ones = jnp.ones((BT, DH), jnp.bfloat16)

    def rows_of(offset):
        return pl.ds(pl.multiple_of((local + BAND + offset) * BT, BT), BT)

    def value_of(offset):
        return jnp.concatenate([values_ref[rows_of(offset), :], ones], axis=1)

    scores = pair_scores(query, keys_ref[rows_of(0), :], bias_ref[2])
    top = row_max(scores)
    max_ref[...] = top
    acc_ref2[...] = weighted(jnp.exp2(scores - top), value_of(0))

    for distance in range(1, BAND + 1):

        @pl.when(reach >= distance)
        def _():
            low = slope * jnp.where(block >= distance, float(distance * BT), FAR_AWAY)
            high = slope * jnp.where(block + distance < total_blocks, float(distance * BT), FAR_AWAY)
            first = pair_scores(query, keys_ref[rows_of(-distance), :], bias_ref[0])
            second = pair_scores(query, keys_ref[rows_of(distance), :], bias_ref[1])
            old = max_ref[...]
            top = jnp.maximum(old, jnp.maximum(row_max(first) - low, row_max(second) - high))
            shrink = jnp.exp2(old - top)
            max_ref[...] = top
            acc_ref2[...] = (
                acc_ref2[...] * shrink
                + weighted(jnp.exp2(first - (top + low)), value_of(-distance))
                + weighted(jnp.exp2(second - (top + high)), value_of(distance))
            )

    total = acc_ref2[:, DH:]
    acc_ref[...] = acc_ref2[:, :DH] / total
    stat_ref[...] = max_ref[...] + jnp.log2(total)


def band_attention(meta, slopes, queries, key_rows, value_rows, before, after, total_blocks):
    tok_rows, channels = queries.shape
    blk_dev = tok_rows // BT
    heads = channels // DH
    any_spec = pl.BlockSpec(memory_space=pltpu.HBM)
    tile = pl.BlockSpec((BT, DH), lambda h, i, *_: (i, h))
    ext = tok_rows + 2 * BAND * BT
    return pl.pallas_call(
        functools.partial(band_kernel, blk_dev=blk_dev, total_blocks=total_blocks),
        out_shape=(
            jax.ShapeDtypeStruct((tok_rows, channels), jnp.float32),
            jax.ShapeDtypeStruct((tok_rows, channels), jnp.float32),
        ),
        grid_spec=pltpu.PrefetchScalarGridSpec(
            num_scalar_prefetch=2,
            grid=(heads, blk_dev),
            in_specs=[tile, any_spec, any_spec, any_spec, any_spec],
            out_specs=(tile, tile),
            scratch_shapes=[
                pltpu.VMEM((ext, DH), jnp.bfloat16),
                pltpu.VMEM((ext, DH), jnp.bfloat16),
                pltpu.VMEM((3, BT, BT), jnp.float32),
                pltpu.VMEM((BT, 1), jnp.float32),
                pltpu.VMEM((BT, 2 * DH), jnp.float32),
                pltpu.SemaphoreType.DMA((2, 3)),
            ],
        ),
        compiler_params=pltpu.CompilerParams(vmem_limit_bytes=12 * MIB),
        cost_estimate=pl.CostEstimate(
            flops=7 * 4 * tok_rows * BT * channels,
            transcendentals=7 * tok_rows * BT * heads,
            bytes_accessed=30 * MIB,
        ),
        name="band",
    )(meta, slopes, queries, key_rows, value_rows, before, after)


def gather_pieces(pieces, buffer_ref, sems, sources):
    if len(pieces) == 1:
        pieces = [pieces[0].at[s] for s in range(sources)]
    copies = [
        pltpu.make_async_copy(piece, buffer_ref.at[s], sems.at[s])
        for s, piece in enumerate(pieces)
    ]
    for copy in copies:
        copy.start()
    return copies


def place_of(slot, me, sources, split):
    source = lax.div(slot, CAP)
    if split:
        source = me - source
        source = jnp.where(source < 0, source + sources, source)
    return source, lax.rem(slot, CAP)


def far_kernel(
    meta_ref, slot_ref, block_ref, slopes_ref, query_ref, acc_ref, stat_ref, *refs, head, blk_dev,
    sources, group, split,
):
    if split:
        pieces = refs[:-6]
        weights_ref, out_ref, scale_ref, buffer_ref, bias_ref, sems = refs[-6:]
    else:
        pieces = refs[:-4]
        out_ref, buffer_ref, bias_ref, sems = refs[-4:]
    local = pl.program_id(0)
    slope = slopes_ref[head] * LOG2E

    @pl.when(local == 0)
    def _():
        copies = gather_pieces(pieces, buffer_ref, sems, sources)
        fill_bias(bias_ref, slope)
        for copy in copies:
            copy.wait()

    me = meta_ref[blk_dev]
    ones = jnp.ones((BT, DH), jnp.bfloat16)
    for part in range(group):
        i = local * group + part
        rows = pl.ds(part * BT, BT)
        block = me * blk_dev + i
        query = query_ref[rows, :]
        scores, values, shifts = [], [], []
        for f in range(FAR):
            apart = block - block_ref[f, i]
            sign = jnp.where(apart > 0, 0, jnp.where(apart < 0, 1, 2))
            shifts.append(slope * (jnp.abs(apart) * BT).astype(jnp.float32))
            source, rank = place_of(slot_ref[f, i], me, sources, split)
            key = buffer_ref[source, rank if split else rank * 2]
            scores.append(pair_scores(query, key, bias_ref[sign]))
            if split:
                values.append(ones)
            else:
                values.append(jnp.concatenate([buffer_ref[source, rank * 2 + 1], ones], axis=1))
        band = stat_ref[rows, :]
        top = jnp.maximum(
            band[:, 0:1],
            jnp.maximum(row_max(scores[0]) - shifts[0], row_max(scores[1]) - shifts[1]),
        )
        weights = [
            jnp.exp2(score - (top + shift)).astype(jnp.bfloat16)
            for score, shift in zip(scores, shifts)
        ]
        far = weighted(weights[0], values[0]) + weighted(weights[1], values[1])
        share = jnp.exp2(band - top)
        scale = 1.0 / (share + far[:, -DH:])
        acc = acc_ref[rows, :] * share
        if split:
            for f in range(FAR):
                weights_ref[rows, f * BT : (f + 1) * BT] = weights[f]
            out_ref[rows, :] = acc
            scale_ref[rows, :] = scale
        else:
            out_ref[rows, :] = ((acc + far[:, :DH]) * scale).astype(jnp.bfloat16)


def far_attention(meta, slots, far_blocks, slopes, queries, acc, stat, pieces, head, sources):
    tok_rows = queries.shape[0]
    blk_dev = tok_rows // BT
    split = len(pieces) > 1
    group = 2 if blk_dev % 2 == 0 else 1
    tile = pl.BlockSpec((group * BT, DH), lambda i, *_: (i, head))
    hbm = pl.BlockSpec(memory_space=pltpu.HBM)
    out_shape = [jax.ShapeDtypeStruct((tok_rows, DH), jnp.float32 if split else jnp.bfloat16)]
    out_specs = [pl.BlockSpec((group * BT, DH), lambda i, *_: (i, 0))]
    if split:
        out_shape = [
            pltpu.VMEM((tok_rows, FAR * BT), jnp.bfloat16),
            pltpu.VMEM((tok_rows, DH), jnp.float32),
            pltpu.VMEM((tok_rows, DH), jnp.float32),
        ]
        out_specs.append(out_specs[0])
        out_specs.insert(0, pl.BlockSpec((group * BT, FAR * BT), lambda i, *_: (i, 0)))
    return pl.pallas_call(
        functools.partial(
            far_kernel, head=head, blk_dev=blk_dev, sources=sources, group=group, split=split
        ),
        out_shape=out_shape,
        grid_spec=pltpu.PrefetchScalarGridSpec(
            num_scalar_prefetch=4,
            grid=(blk_dev // group,),
            in_specs=[tile, tile, tile] + [hbm] * len(pieces),
            out_specs=out_specs,
            scratch_shapes=[
                pltpu.VMEM((sources, CAP if split else CAP * 2, BT, DH), jnp.bfloat16),
                pltpu.VMEM((3, BT, BT), jnp.float32),
                pltpu.SemaphoreType.DMA((sources,)),
            ],
        ),
        compiler_params=pltpu.CompilerParams(vmem_limit_bytes=14 * MIB),
        cost_estimate=pl.CostEstimate(
            flops=2 * 4 * tok_rows * BT * DH,
            transcendentals=2 * tok_rows * BT,
            bytes_accessed=14 * MIB,
        ),
        name="far",
    )(meta, slots, far_blocks, slopes, queries, acc, stat, *pieces)


def value_kernel(me_ref, slot_ref, weights_ref, acc_ref, scale_ref, *refs, sources, blk_dev):
    pieces = refs[:-3]
    out_ref, buffer_ref, sems = refs[-3:]
    for copy in gather_pieces(pieces, buffer_ref, sems, sources):
        copy.wait()
    for i in range(blk_dev):
        r = pl.ds(i * BT, BT)
        acc = acc_ref[r, :]
        for f in range(FAR):
            source, rank = place_of(slot_ref[f, i], me_ref[0], sources, True)
            acc = acc + weighted(weights_ref[r, f * BT : (f + 1) * BT], buffer_ref[source, rank])
        out_ref[r, :] = (acc * scale_ref[r, :]).astype(jnp.bfloat16)


def far_values(me, slots, weights, acc, scale, pieces, sources):
    tok_rows = acc.shape[0]
    blk_dev = tok_rows // BT
    smem = pl.BlockSpec(memory_space=pltpu.SMEM)
    vmem = pl.BlockSpec(memory_space=pltpu.VMEM)
    hbm = pl.BlockSpec(memory_space=pltpu.HBM)
    return pl.pallas_call(
        functools.partial(value_kernel, sources=sources, blk_dev=blk_dev),
        out_shape=pltpu.VMEM((tok_rows, DH), jnp.bfloat16),
        in_specs=[smem, smem] + [vmem] * 3 + [hbm] * len(pieces),
        out_specs=vmem,
        scratch_shapes=[
            pltpu.VMEM((sources, CAP, BT, DH), jnp.bfloat16),
            pltpu.SemaphoreType.DMA((sources,)),
        ],
        compiler_params=pltpu.CompilerParams(vmem_limit_bytes=4 * MIB),
        name="values",
    )(me, slots, weights, acc, scale, *pieces)


def place_kernel(*refs, heads):
    parts = refs[:heads]
    out_ref, sems = refs[heads:]
    peers = parts[0].shape[0]
    width = heads * DH
    copies = [
        pltpu.make_async_copy(
            part.at[g], out_ref.at[:, pl.ds(g * width + head * DH, DH)], sems.at[g, head]
        )
        for head, part in enumerate(parts)
        for g in range(peers)
    ]
    for copy in copies:
        copy.start()
    for copy in copies:
        copy.wait()


def place(parts):
    peers, rows, _ = parts[0].shape
    heads = len(parts)
    return pl.pallas_call(
        functools.partial(place_kernel, heads=heads),
        out_shape=jax.ShapeDtypeStruct((rows, peers * heads * DH), parts[0].dtype),
        in_specs=[pl.BlockSpec(memory_space=pltpu.VMEM)] * heads,
        out_specs=pl.BlockSpec(memory_space=pltpu.HBM),
        scratch_shapes=[pltpu.SemaphoreType.DMA((peers, heads))],
        name="place",
    )(*(pltpu.with_memory_space_constraint(part, pltpu.VMEM) for part in parts))


def body(queries, key_rows, value_rows, band_reach, far_list, slopes):
    myself = lax.axis_index("seq")
    sources = lax.axis_size("seq")
    tok_rows, channels = key_rows.shape
    blk_dev = tok_rows // BT
    margin = BAND * BT
    heads = channels // DH
    up = [(i, i + 1) for i in range(sources - 1)]
    down = [(i + 1, i) for i in range(sources - 1)]

    table, slots = route(far_list, sources)
    asked = lax.all_to_all(table, "seq", split_axis=0, concat_axis=0, tiled=True)
    last = jnp.stack([key_rows[tok_rows - margin :], value_rows[tok_rows - margin :]])
    first = jnp.stack([key_rows[:margin], value_rows[:margin]])
    before = lax.ppermute(last, "seq", up)
    after = lax.ppermute(first, "seq", down)

    me = myself[None].astype(jnp.int32)
    keys_hbm, values_hbm = (
        pltpu.with_memory_space_constraint(x, pltpu.HBM) for x in (key_rows, value_rows)
    )
    incoming = []
    for head in range(heads):
        split = head == heads - 1
        outgoing = pack(asked, me, keys_hbm, values_hbm, head, split)
        if split:
            pieces = []
            for which in range(2):
                arrays = list(outgoing[which * sources : (which + 1) * sources])
                for shift in range(1, sources):
                    ring = [(i, (i + shift) % sources) for i in range(sources)]
                    arrays[shift] = lax.ppermute(arrays[shift], "seq", ring)
                pieces.append([pltpu.with_memory_space_constraint(x, pltpu.HBM) for x in arrays])
            incoming.append(pieces)
        else:
            incoming.append(
                [lax.all_to_all(outgoing[0], "seq", split_axis=0, concat_axis=0, tiled=True)]
            )

    meta = jnp.concatenate([band_reach, me])
    acc, stat = band_attention(
        meta, slopes, queries, key_rows, value_rows, before, after, blk_dev * sources
    )
    acc, stat, queries = (
        pltpu.with_memory_space_constraint(x, pltpu.HBM) for x in (acc, stat, queries)
    )
    parts = []
    for head in range(heads):
        split = head == heads - 1
        pieces = incoming[head][0] if split else incoming[head]
        attended = far_attention(
            meta, slots, far_list.T, slopes, queries, acc, stat, pieces, head, sources
        )
        if split:
            attended = far_values(me, slots, *attended, incoming[head][1], sources)
        else:
            attended = attended[0]
        parts.append(
            lax.all_to_all(
                attended.reshape(lax.axis_size("head"), -1, DH), "head",
                split_axis=0, concat_axis=0, tiled=True,
            )
        )
    return place(parts)


def solution(mesh):
    in_specs = (
        P("seq", "head"),
        P("seq", "head"),
        P("seq", "head"),
        P("seq"),
        P("seq", None),
        P("head"),
    )
    out_specs = P(("seq", "head"), None)

    return jax.shard_map(body, mesh=mesh, in_specs=in_specs, out_specs=out_specs, check_vma=False)
```

```python
import functools
import math

import jax
import jax.numpy as jnp
from jax import lax
from jax.experimental import pallas as pl
from jax.experimental.pallas import tpu as pltpu
from jax.sharding import PartitionSpec as P


BT = 256
BAND = 3
FAR = 2
CAP = 2
DH = 128
LOG2E = 1.4426950408889634
FAR_AWAY = 1e30
MIB = 1 << 20


def route_kernel(
    far_ref, keys_hbm, values_hbm, table_ref, slot_ref, last_ref, first_ref, count_ref, sems,
    *, sources, blk_dev,
):
    margin = BAND * BT
    copies = []
    for which, ref in enumerate((keys_hbm, values_hbm)):
        copies += [
            pltpu.make_async_copy(
                ref.at[pl.ds(blk_dev * BT - margin, margin)], last_ref.at[which], sems.at[which, 0]
            ),
            pltpu.make_async_copy(ref.at[pl.ds(0, margin)], first_ref.at[which], sems.at[which, 1]),
        ]
    for copy in copies:
        copy.start()
    for s in range(sources):
        count_ref[s] = 0
        for r in range(CAP):
            table_ref[s, r] = 0

    def step(i, carry):
        for f in range(FAR):
            block = far_ref[f, i]
            s = lax.div(block, blk_dev)
            r = jnp.minimum(count_ref[s], CAP - 1)
            count_ref[s] = r + 1
            table_ref[s, r] = block - s * blk_dev
            slot_ref[f, i] = s * CAP + r
        return carry

    lax.fori_loop(0, blk_dev, step, 0)
    for copy in copies:
        copy.wait()


def route(far_list, key_rows, value_rows, sources):
    blk_dev = far_list.shape[0]
    smem = pl.BlockSpec(memory_space=pltpu.SMEM)
    vmem = pl.BlockSpec(memory_space=pltpu.VMEM)
    hbm = pl.BlockSpec(memory_space=pltpu.HBM)
    halo = pltpu.VMEM((2, BAND * BT, key_rows.shape[1]), key_rows.dtype)
    return pl.pallas_call(
        functools.partial(route_kernel, sources=sources, blk_dev=blk_dev),
        out_shape=(
            jax.ShapeDtypeStruct((sources, CAP), jnp.int32),
            jax.ShapeDtypeStruct((FAR, blk_dev), jnp.int32),
            halo,
            halo,
        ),
        in_specs=[smem, hbm, hbm],
        out_specs=(smem, smem, vmem, vmem),
        scratch_shapes=[pltpu.SMEM((sources,), jnp.int32), pltpu.SemaphoreType.DMA((2, 2))],
        compiler_params=pltpu.CompilerParams(vmem_limit_bytes=4 * MIB),
        name="route",
    )(far_list.T, key_rows, value_rows)


def pack_kernel(asked_ref, me_ref, keys_ref, values_ref, *refs, shifts):
    out_refs, sems = refs[:-1], refs[-1]
    copies = []
    for which, ref in enumerate((keys_ref, values_ref)):
        for shift in range(shifts):
            target = me_ref[0] + shift
            target = jnp.where(target >= shifts, target - shifts, target)
            for r in range(CAP):
                rows = pl.ds(pl.multiple_of(asked_ref[target, r] * BT, BT), BT)
                slot = r * 2 + which
                if len(out_refs) == 1:
                    dst = out_refs[0].at[target, slot]
                else:
                    dst = out_refs[which * shifts + shift].at[r]
                copy = pltpu.make_async_copy(ref.at[rows, :], dst, sems.at[shift, slot])
                copy.start()
                copies.append(copy)
    for copy in copies:
        copy.wait()


def pack(asked, me, key_rows, value_rows, head, split):
    shifts = asked.shape[0]
    tok_rows = key_rows.shape[0]
    hbm = pl.BlockSpec(memory_space=pltpu.HBM)
    column = pl.BlockSpec((tok_rows, DH), lambda i, *_: (0, head))
    if split:
        out_shape = (pltpu.HBM((CAP, BT, DH), key_rows.dtype),) * (2 * shifts)
    else:
        out_shape = (pltpu.HBM((shifts, CAP * 2, BT, DH), key_rows.dtype),)
    return pl.pallas_call(
        functools.partial(pack_kernel, shifts=shifts),
        out_shape=out_shape,
        grid_spec=pltpu.PrefetchScalarGridSpec(
            num_scalar_prefetch=2,
            grid=(1,),
            in_specs=[column, column],
            out_specs=(hbm,) * len(out_shape),
            scratch_shapes=[pltpu.SemaphoreType.DMA((shifts, CAP * 2))],
        ),
        compiler_params=pltpu.CompilerParams(vmem_limit_bytes=16 * MIB),
        name="pack",
    )(asked, me, key_rows, value_rows)


def fill_bias(bias_ref, slope):
    rows = lax.broadcasted_iota(jnp.int32, (BT, BT), 0)
    columns = lax.broadcasted_iota(jnp.int32, (BT, BT), 1)
    gap = (rows - columns).astype(jnp.float32) * slope
    bias_ref[0] = gap
    bias_ref[1] = -gap
    bias_ref[2] = jnp.abs(gap)


def pair_scores(query, key, bias):
    product = lax.dot_general(
        query, key, (((1,), (1,)), ((), ())), preferred_element_type=jnp.float32
    )
    return product * (LOG2E / math.sqrt(DH)) - bias


def weighted(weights, value):
    return lax.dot_general(
        weights.astype(jnp.bfloat16), value, (((1,), (0,)), ((), ())),
        preferred_element_type=jnp.float32,
    )


def row_max(scores):
    return jnp.max(scores, axis=1, keepdims=True)


def band_kernel(
    meta_ref, slopes_ref, query_ref, keys_hbm, values_hbm, before_hbm, after_hbm,
    acc_ref, stat_ref,
    keys_ref, values_ref, bias_ref, max_ref, acc_ref2, sems, *, blk_dev, total_blocks,
):
    head = pl.program_id(0)
    local = pl.program_id(1)
    margin = BAND * BT
    tok_rows = blk_dev * BT
    slope = slopes_ref[head] * LOG2E

    @pl.when(local == 0)
    def _():
        column = pl.ds(pl.multiple_of(head * DH, DH), DH)
        copies = []
        for which, (ref, whole) in enumerate(((keys_ref, keys_hbm), (values_ref, values_hbm))):
            copies += [
                pltpu.make_async_copy(
                    before_hbm.at[which, :, column], ref.at[pl.ds(0, margin)], sems.at[which, 0]
                ),
                pltpu.make_async_copy(
                    whole.at[:, column], ref.at[pl.ds(margin, tok_rows)], sems.at[which, 1]
                ),
                pltpu.make_async_copy(
                    after_hbm.at[which, :, column],
                    ref.at[pl.ds(margin + tok_rows, margin)],
                    sems.at[which, 2],
                ),
            ]
        for copy in copies:
            copy.start()
        fill_bias(bias_ref, slope)
        for copy in copies:
            copy.wait()

    reach = meta_ref[local]
    block = meta_ref[blk_dev] * blk_dev + local
    query = query_ref[...]
    ones = jnp.ones((BT, DH), jnp.bfloat16)

    def rows_of(offset):
        return pl.ds(pl.multiple_of((local + BAND + offset) * BT, BT), BT)

    def value_of(offset):
        return jnp.concatenate([values_ref[rows_of(offset), :], ones], axis=1)

    scores = pair_scores(query, keys_ref[rows_of(0), :], bias_ref[2])
    top = row_max(scores)
    max_ref[...] = top
    acc_ref2[...] = weighted(jnp.exp2(scores - top), value_of(0))

    for distance in range(1, BAND + 1):

        @pl.when(reach >= distance)
        def _():
            low = slope * jnp.where(block >= distance, float(distance * BT), FAR_AWAY)
            high = slope * jnp.where(block + distance < total_blocks, float(distance * BT), FAR_AWAY)
            first = pair_scores(query, keys_ref[rows_of(-distance), :], bias_ref[0])
            second = pair_scores(query, keys_ref[rows_of(distance), :], bias_ref[1])
            old = max_ref[...]
            top = jnp.maximum(old, jnp.maximum(row_max(first) - low, row_max(second) - high))
            shrink = jnp.exp2(old - top)
            max_ref[...] = top
            acc_ref2[...] = (
                acc_ref2[...] * shrink
                + weighted(jnp.exp2(first - (top + low)), value_of(-distance))
                + weighted(jnp.exp2(second - (top + high)), value_of(distance))
            )

    total = acc_ref2[:, DH:]
    acc_ref[...] = acc_ref2[:, :DH] / total
    stat_ref[...] = max_ref[...] + jnp.log2(total)


def band_attention(meta, slopes, queries, key_rows, value_rows, before, after, total_blocks):
    tok_rows, channels = queries.shape
    blk_dev = tok_rows // BT
    heads = channels // DH
    any_spec = pl.BlockSpec(memory_space=pltpu.HBM)
    tile = pl.BlockSpec((BT, DH), lambda h, i, *_: (i, h))
    ext = tok_rows + 2 * BAND * BT
    return pl.pallas_call(
        functools.partial(band_kernel, blk_dev=blk_dev, total_blocks=total_blocks),
        out_shape=(
            jax.ShapeDtypeStruct((tok_rows, channels), jnp.float32),
            jax.ShapeDtypeStruct((tok_rows, channels), jnp.float32),
        ),
        grid_spec=pltpu.PrefetchScalarGridSpec(
            num_scalar_prefetch=2,
            grid=(heads, blk_dev),
            in_specs=[tile, any_spec, any_spec, any_spec, any_spec],
            out_specs=(tile, tile),
            scratch_shapes=[
                pltpu.VMEM((ext, DH), jnp.bfloat16),
                pltpu.VMEM((ext, DH), jnp.bfloat16),
                pltpu.VMEM((3, BT, BT), jnp.float32),
                pltpu.VMEM((BT, 1), jnp.float32),
                pltpu.VMEM((BT, 2 * DH), jnp.float32),
                pltpu.SemaphoreType.DMA((2, 3)),
            ],
        ),
        compiler_params=pltpu.CompilerParams(vmem_limit_bytes=12 * MIB),
        cost_estimate=pl.CostEstimate(
            flops=7 * 4 * tok_rows * BT * channels,
            transcendentals=7 * tok_rows * BT * heads,
            bytes_accessed=30 * MIB,
        ),
        name="band",
    )(meta, slopes, queries, key_rows, value_rows, before, after)


def gather_pieces(pieces, buffer_ref, sems, sources):
    if len(pieces) == 1:
        pieces = [pieces[0].at[s] for s in range(sources)]
    copies = [
        pltpu.make_async_copy(piece, buffer_ref.at[s], sems.at[s])
        for s, piece in enumerate(pieces)
    ]
    for copy in copies:
        copy.start()
    return copies


def place_of(slot, me, sources, split):
    source = lax.div(slot, CAP)
    if split:
        source = me - source
        source = jnp.where(source < 0, source + sources, source)
    return source, lax.rem(slot, CAP)


def far_kernel(
    meta_ref, slot_ref, block_ref, slopes_ref, query_ref, acc_ref, stat_ref, *refs, head, blk_dev,
    sources, group, split,
):
    if split:
        pieces = refs[:-6]
        weights_ref, out_ref, scale_ref, buffer_ref, bias_ref, sems = refs[-6:]
    else:
        pieces = refs[:-4]
        out_ref, buffer_ref, bias_ref, sems = refs[-4:]
    local = pl.program_id(0)
    slope = slopes_ref[head] * LOG2E

    @pl.when(local == 0)
    def _():
        copies = gather_pieces(pieces, buffer_ref, sems, sources)
        fill_bias(bias_ref, slope)
        for copy in copies:
            copy.wait()

    me = meta_ref[blk_dev]
    ones = jnp.ones((BT, DH), jnp.bfloat16)
    for part in range(group):
        i = local * group + part
        rows = pl.ds(part * BT, BT)
        block = me * blk_dev + i
        query = query_ref[rows, :]
        scores, values, shifts = [], [], []
        for f in range(FAR):
            apart = block - block_ref[f, i]
            sign = jnp.where(apart > 0, 0, jnp.where(apart < 0, 1, 2))
            shifts.append(slope * (jnp.abs(apart) * BT).astype(jnp.float32))
            source, rank = place_of(slot_ref[f, i], me, sources, split)
            key = buffer_ref[source, rank if split else rank * 2]
            scores.append(pair_scores(query, key, bias_ref[sign]))
            if split:
                values.append(ones)
            else:
                values.append(jnp.concatenate([buffer_ref[source, rank * 2 + 1], ones], axis=1))
        band = stat_ref[rows, :]
        top = jnp.maximum(
            band[:, 0:1],
            jnp.maximum(row_max(scores[0]) - shifts[0], row_max(scores[1]) - shifts[1]),
        )
        weights = [
            jnp.exp2(score - (top + shift)).astype(jnp.bfloat16)
            for score, shift in zip(scores, shifts)
        ]
        far = weighted(weights[0], values[0]) + weighted(weights[1], values[1])
        share = jnp.exp2(band - top)
        scale = 1.0 / (share + far[:, -DH:])
        acc = acc_ref[rows, :] * share
        if split:
            for f in range(FAR):
                weights_ref[rows, f * BT : (f + 1) * BT] = weights[f]
            out_ref[rows, :] = acc
            scale_ref[rows, :] = scale
        else:
            out_ref[rows, :] = ((acc + far[:, :DH]) * scale).astype(jnp.bfloat16)


def far_attention(meta, slots, far_blocks, slopes, queries, acc, stat, pieces, head, sources):
    tok_rows = queries.shape[0]
    blk_dev = tok_rows // BT
    split = len(pieces) > 1
    group = 2 if blk_dev % 2 == 0 else 1
    tile = pl.BlockSpec((group * BT, DH), lambda i, *_: (i, head))
    hbm = pl.BlockSpec(memory_space=pltpu.HBM)
    out_shape = [jax.ShapeDtypeStruct((tok_rows, DH), jnp.float32 if split else jnp.bfloat16)]
    out_specs = [pl.BlockSpec((group * BT, DH), lambda i, *_: (i, 0))]
    if split:
        out_shape = [
            pltpu.VMEM((tok_rows, FAR * BT), jnp.bfloat16),
            pltpu.VMEM((tok_rows, DH), jnp.float32),
            pltpu.VMEM((tok_rows, DH), jnp.float32),
        ]
        out_specs.append(out_specs[0])
        out_specs.insert(0, pl.BlockSpec((group * BT, FAR * BT), lambda i, *_: (i, 0)))
    return pl.pallas_call(
        functools.partial(
            far_kernel, head=head, blk_dev=blk_dev, sources=sources, group=group, split=split
        ),
        out_shape=out_shape,
        grid_spec=pltpu.PrefetchScalarGridSpec(
            num_scalar_prefetch=4,
            grid=(blk_dev // group,),
            in_specs=[tile, tile, tile] + [hbm] * len(pieces),
            out_specs=out_specs,
            scratch_shapes=[
                pltpu.VMEM((sources, CAP if split else CAP * 2, BT, DH), jnp.bfloat16),
                pltpu.VMEM((3, BT, BT), jnp.float32),
                pltpu.SemaphoreType.DMA((sources,)),
            ],
        ),
        compiler_params=pltpu.CompilerParams(vmem_limit_bytes=14 * MIB),
        cost_estimate=pl.CostEstimate(
            flops=2 * 4 * tok_rows * BT * DH,
            transcendentals=2 * tok_rows * BT,
            bytes_accessed=14 * MIB,
        ),
        name="far",
    )(meta, slots, far_blocks, slopes, queries, acc, stat, *pieces)


def value_kernel(me_ref, slot_ref, weights_ref, acc_ref, scale_ref, *refs, sources, blk_dev):
    pieces = refs[:-2]
    out_ref, buffer_ref = refs[-2:]
    for s, piece in enumerate(pieces):
        buffer_ref[s] = piece[...]
    for i in range(blk_dev):
        r = pl.ds(i * BT, BT)
        acc = acc_ref[r, :]
        for f in range(FAR):
            source, rank = place_of(slot_ref[f, i], me_ref[0], sources, True)
            acc = acc + weighted(weights_ref[r, f * BT : (f + 1) * BT], buffer_ref[source, rank])
        out_ref[r, :] = (acc * scale_ref[r, :]).astype(jnp.bfloat16)


def far_values(me, slots, weights, acc, scale, pieces, sources):
    tok_rows = acc.shape[0]
    blk_dev = tok_rows // BT
    smem = pl.BlockSpec(memory_space=pltpu.SMEM)
    vmem = pl.BlockSpec(memory_space=pltpu.VMEM)
    return pl.pallas_call(
        functools.partial(value_kernel, sources=sources, blk_dev=blk_dev),
        out_shape=pltpu.VMEM((tok_rows, DH), jnp.bfloat16),
        in_specs=[smem, smem] + [vmem] * (3 + len(pieces)),
        out_specs=vmem,
        scratch_shapes=[pltpu.VMEM((sources, CAP, BT, DH), jnp.bfloat16)],
        compiler_params=pltpu.CompilerParams(vmem_limit_bytes=4 * MIB),
        name="values",
    )(me, slots, weights, acc, scale, *pieces)


def place_kernel(*refs, heads):
    parts = refs[:heads]
    out_ref, sems = refs[heads:]
    peers = parts[0].shape[0]
    width = heads * DH
    copies = [
        pltpu.make_async_copy(
            part.at[g], out_ref.at[:, pl.ds(g * width + head * DH, DH)], sems.at[g, head]
        )
        for head, part in enumerate(parts)
        for g in range(peers)
    ]
    for copy in copies:
        copy.start()
    for copy in copies:
        copy.wait()


def place(parts):
    peers, rows, _ = parts[0].shape
    heads = len(parts)
    return pl.pallas_call(
        functools.partial(place_kernel, heads=heads),
        out_shape=jax.ShapeDtypeStruct((rows, peers * heads * DH), parts[0].dtype),
        in_specs=[pl.BlockSpec(memory_space=pltpu.VMEM)] * heads,
        out_specs=pl.BlockSpec(memory_space=pltpu.HBM),
        scratch_shapes=[pltpu.SemaphoreType.DMA((peers, heads))],
        name="place",
    )(*(pltpu.with_memory_space_constraint(part, pltpu.VMEM) for part in parts))


def body(queries, key_rows, value_rows, band_reach, far_list, slopes):
    myself = lax.axis_index("seq")
    sources = lax.axis_size("seq")
    tok_rows, channels = key_rows.shape
    blk_dev = tok_rows // BT
    heads = channels // DH
    up = [(i, i + 1) for i in range(sources - 1)]
    down = [(i + 1, i) for i in range(sources - 1)]

    keys_hbm, values_hbm = (
        pltpu.with_memory_space_constraint(x, pltpu.HBM) for x in (key_rows, value_rows)
    )
    table, slots, last, first = route(far_list, keys_hbm, values_hbm, sources)
    asked = lax.all_to_all(table, "seq", split_axis=0, concat_axis=0, tiled=True)
    before = lax.ppermute(last, "seq", up)
    after = lax.ppermute(first, "seq", down)

    me = myself[None].astype(jnp.int32)
    incoming = []
    for head in range(heads):
        split = head == heads - 1
        outgoing = pack(asked, me, keys_hbm, values_hbm, head, split)
        if split:
            pieces = []
            for which, kind in enumerate(("key", "value")):
                arrays = list(outgoing[which * sources : (which + 1) * sources])
                for shift in range(1, sources):
                    ring = [(i, (i + shift) % sources) for i in range(sources)]
                    arrays[shift] = lax.ppermute(arrays[shift], "seq", ring)
                space = pltpu.HBM if kind == "key" else pltpu.VMEM
                pieces.append([pltpu.with_memory_space_constraint(x, space) for x in arrays])
            incoming.append(pieces)
        else:
            incoming.append(
                [lax.all_to_all(outgoing[0], "seq", split_axis=0, concat_axis=0, tiled=True)]
            )

    meta = jnp.concatenate([band_reach, me])
    acc, stat = band_attention(
        meta, slopes, queries, key_rows, value_rows, before, after, blk_dev * sources
    )
    acc, stat, queries = (
        pltpu.with_memory_space_constraint(x, pltpu.HBM) for x in (acc, stat, queries)
    )
    parts = []
    for head in range(heads):
        split = head == heads - 1
        pieces = incoming[head][0] if split else incoming[head]
        attended = far_attention(
            meta, slots, far_list.T, slopes, queries, acc, stat, pieces, head, sources
        )
        if split:
            attended = far_values(me, slots, *attended, incoming[head][1], sources)
        else:
            attended = attended[0]
        parts.append(
            lax.all_to_all(
                attended.reshape(lax.axis_size("head"), -1, DH), "head",
                split_axis=0, concat_axis=0, tiled=True,
            )
        )
    return place(parts)


def solution(mesh):
    in_specs = (
        P("seq", "head"),
        P("seq", "head"),
        P("seq", "head"),
        P("seq"),
        P("seq", None),
        P("head"),
    )
    out_specs = P(("seq", "head"), None)

    return jax.shard_map(body, mesh=mesh, in_specs=in_specs, out_specs=out_specs, check_vma=False)
```

```python
import functools
import math

import jax
import jax.numpy as jnp
from jax import lax
from jax.experimental import pallas as pl
from jax.experimental.pallas import tpu as pltpu
from jax.sharding import PartitionSpec as P


BT = 256
BAND = 3
FAR = 2
CAP = 2
DH = 128
LOG2E = 1.4426950408889634
FAR_AWAY = 1e30
MIB = 1 << 20


def route_kernel(far_ref, table_ref, slot_ref, count_ref, *, sources, blk_dev):
    for s in range(sources):
        count_ref[s] = 0
        for r in range(CAP):
            table_ref[s, r] = 0

    def step(i, carry):
        for f in range(FAR):
            block = far_ref[f, i]
            s = lax.div(block, blk_dev)
            r = jnp.minimum(count_ref[s], CAP - 1)
            count_ref[s] = r + 1
            table_ref[s, r] = block - s * blk_dev
            slot_ref[f, i] = s * CAP + r
        return carry

    lax.fori_loop(0, blk_dev, step, 0)


def route(far_list, sources):
    blk_dev = far_list.shape[0]
    smem = pl.BlockSpec(memory_space=pltpu.SMEM)
    return pl.pallas_call(
        functools.partial(route_kernel, sources=sources, blk_dev=blk_dev),
        out_shape=(
            jax.ShapeDtypeStruct((sources, CAP), jnp.int32),
            jax.ShapeDtypeStruct((FAR, blk_dev), jnp.int32),
        ),
        in_specs=[smem],
        out_specs=(smem, smem),
        scratch_shapes=[pltpu.SMEM((sources,), jnp.int32)],
        name="route",
    )(pltpu.with_memory_space_constraint(far_list.T, pltpu.HBM))


def stage_kernel(*refs, moves):
    sources, targets, sems = refs[:2], refs[2:-1], refs[-1]
    copies = [
        pltpu.make_async_copy(sources[which].at[rows, columns], target, sems.at[i])
        for i, (which, rows, columns, target) in enumerate(moves(targets))
    ]
    for copy in copies:
        copy.start()
    for copy in copies:
        copy.wait()


def stage(key_rows, value_rows, shapes, moves, count):
    vmem = pl.BlockSpec(memory_space=pltpu.VMEM)
    hbm = pl.BlockSpec(memory_space=pltpu.HBM)
    staged = pl.pallas_call(
        functools.partial(stage_kernel, moves=moves),
        out_shape=tuple(pltpu.VMEM(shape, key_rows.dtype) for shape in shapes),
        in_specs=[hbm, hbm],
        out_specs=(vmem,) * len(shapes),
        scratch_shapes=[pltpu.SemaphoreType.DMA((count,))],
        compiler_params=pltpu.CompilerParams(vmem_limit_bytes=4 * MIB),
    )(key_rows, value_rows)
    return [pltpu.with_memory_space_constraint(x, pltpu.VMEM) for x in staged]


def halos(key_rows, value_rows):
    tok_rows, channels = key_rows.shape
    margin = BAND * BT
    whole = pl.ds(0, channels)

    def moves(targets):
        return [
            (which, pl.ds(start, margin), whole, target.at[which])
            for which in range(2)
            for start, target in zip((tok_rows - margin, 0), targets)
        ]

    return stage(key_rows, value_rows, [(2, margin, channels)] * 2, moves, 4)


def head_columns(key_rows, value_rows, head):
    tok_rows = key_rows.shape[0]

    def moves(targets):
        return [
            (which, pl.ds(0, tok_rows), pl.ds(head * DH, DH), target)
            for which, target in enumerate(targets)
        ]

    return stage(key_rows, value_rows, [(tok_rows, DH)] * 2, moves, 2)


def pack_kernel(asked_ref, me_ref, keys_ref, values_ref, *refs, shifts):
    out_refs, sems = refs[:-1], refs[-1]
    copies = []
    for which, ref in enumerate((keys_ref, values_ref)):
        for shift in range(shifts):
            target = me_ref[0] + shift
            target = jnp.where(target >= shifts, target - shifts, target)
            for r in range(CAP):
                rows = pl.ds(pl.multiple_of(asked_ref[target, r] * BT, BT), BT)
                slot = r * 2 + which
                if len(out_refs) == 1:
                    dst = out_refs[0].at[target, slot]
                else:
                    dst = out_refs[which * shifts + shift].at[r]
                copy = pltpu.make_async_copy(ref.at[rows, :], dst, sems.at[shift, slot])
                copy.start()
                copies.append(copy)
    for copy in copies:
        copy.wait()


def pack(asked, me, keys, values, head, split):
    shifts = asked.shape[0]
    tok_rows, channels = keys.shape
    hbm = pl.BlockSpec(memory_space=pltpu.HBM)
    if split:
        out_shape = (pltpu.HBM((CAP, BT, DH), keys.dtype),) * (2 * shifts)
    else:
        out_shape = (pltpu.HBM((shifts, CAP * 2, BT, DH), keys.dtype),)
    scratch = [pltpu.SemaphoreType.DMA((shifts, CAP * 2))]
    if channels == DH:
        smem = pl.BlockSpec(memory_space=pltpu.SMEM)
        vmem = pl.BlockSpec(memory_space=pltpu.VMEM)
        layout = dict(
            in_specs=[smem, smem, vmem, vmem],
            out_specs=(hbm,) * len(out_shape),
            scratch_shapes=scratch,
        )
    else:
        column = pl.BlockSpec((tok_rows, DH), lambda i, *_: (0, head))
        layout = dict(
            grid_spec=pltpu.PrefetchScalarGridSpec(
                num_scalar_prefetch=2,
                grid=(1,),
                in_specs=[column, column],
                out_specs=(hbm,) * len(out_shape),
                scratch_shapes=scratch,
            )
        )
    return pl.pallas_call(
        functools.partial(pack_kernel, shifts=shifts),
        out_shape=out_shape,
        compiler_params=pltpu.CompilerParams(vmem_limit_bytes=16 * MIB),
        name="pack",
        **layout,
    )(asked, me, keys, values)


def fill_bias(bias_ref, slope):
    rows = lax.broadcasted_iota(jnp.int32, (BT, BT), 0)
    columns = lax.broadcasted_iota(jnp.int32, (BT, BT), 1)
    gap = (rows - columns).astype(jnp.float32) * slope
    bias_ref[0] = gap
    bias_ref[1] = -gap
    bias_ref[2] = jnp.abs(gap)


def pair_scores(query, key, bias):
    product = lax.dot_general(
        query, key, (((1,), (1,)), ((), ())), preferred_element_type=jnp.float32
    )
    return product * (LOG2E / math.sqrt(DH)) - bias


def weighted(weights, value):
    return lax.dot_general(
        weights.astype(jnp.bfloat16), value, (((1,), (0,)), ((), ())),
        preferred_element_type=jnp.float32,
    )


def row_max(scores):
    return jnp.max(scores, axis=1, keepdims=True)


def band_kernel(
    meta_ref, slopes_ref, query_ref, keys_hbm, values_hbm, before_hbm, after_hbm,
    acc_ref, stat_ref,
    keys_ref, values_ref, bias_ref, max_ref, acc_ref2, sems, *, blk_dev, total_blocks,
):
    head = pl.program_id(0)
    local = pl.program_id(1)
    margin = BAND * BT
    tok_rows = blk_dev * BT
    slope = slopes_ref[head] * LOG2E

    @pl.when(local == 0)
    def _():
        column = pl.ds(pl.multiple_of(head * DH, DH), DH)
        copies = []
        for which, (ref, whole) in enumerate(((keys_ref, keys_hbm), (values_ref, values_hbm))):
            copies += [
                pltpu.make_async_copy(
                    before_hbm.at[which, :, column], ref.at[pl.ds(0, margin)], sems.at[which, 0]
                ),
                pltpu.make_async_copy(
                    whole.at[:, column], ref.at[pl.ds(margin, tok_rows)], sems.at[which, 1]
                ),
                pltpu.make_async_copy(
                    after_hbm.at[which, :, column],
                    ref.at[pl.ds(margin + tok_rows, margin)],
                    sems.at[which, 2],
                ),
            ]
        for copy in copies:
            copy.start()
        fill_bias(bias_ref, slope)
        for copy in copies:
            copy.wait()

    reach = meta_ref[local]
    block = meta_ref[blk_dev] * blk_dev + local
    query = query_ref[...]
    ones = jnp.ones((BT, DH), jnp.bfloat16)

    def rows_of(offset):
        return pl.ds(pl.multiple_of((local + BAND + offset) * BT, BT), BT)

    def value_of(offset):
        return jnp.concatenate([values_ref[rows_of(offset), :], ones], axis=1)

    scores = pair_scores(query, keys_ref[rows_of(0), :], bias_ref[2])
    top = row_max(scores)
    max_ref[...] = top
    acc_ref2[...] = weighted(jnp.exp2(scores - top), value_of(0))

    for distance in range(1, BAND + 1):

        @pl.when(reach >= distance)
        def _():
            low = slope * jnp.where(block >= distance, float(distance * BT), FAR_AWAY)
            high = slope * jnp.where(block + distance < total_blocks, float(distance * BT), FAR_AWAY)
            first = pair_scores(query, keys_ref[rows_of(-distance), :], bias_ref[0])
            second = pair_scores(query, keys_ref[rows_of(distance), :], bias_ref[1])
            old = max_ref[...]
            top = jnp.maximum(old, jnp.maximum(row_max(first) - low, row_max(second) - high))
            shrink = jnp.exp2(old - top)
            max_ref[...] = top
            acc_ref2[...] = (
                acc_ref2[...] * shrink
                + weighted(jnp.exp2(first - (top + low)), value_of(-distance))
                + weighted(jnp.exp2(second - (top + high)), value_of(distance))
            )

    total = acc_ref2[:, DH:]
    acc_ref[...] = acc_ref2[:, :DH] / total
    stat_ref[...] = max_ref[...] + jnp.log2(total)


def band_attention(meta, slopes, queries, key_rows, value_rows, before, after, total_blocks):
    tok_rows, channels = queries.shape
    blk_dev = tok_rows // BT
    heads = channels // DH
    any_spec = pl.BlockSpec(memory_space=pltpu.HBM)
    tile = pl.BlockSpec((BT, DH), lambda h, i, *_: (i, h))
    ext = tok_rows + 2 * BAND * BT
    return pl.pallas_call(
        functools.partial(band_kernel, blk_dev=blk_dev, total_blocks=total_blocks),
        out_shape=(
            jax.ShapeDtypeStruct((tok_rows, channels), jnp.float32),
            jax.ShapeDtypeStruct((tok_rows, channels), jnp.float32),
        ),
        grid_spec=pltpu.PrefetchScalarGridSpec(
            num_scalar_prefetch=2,
            grid=(heads, blk_dev),
            in_specs=[tile, any_spec, any_spec, any_spec, any_spec],
            out_specs=(tile, tile),
            scratch_shapes=[
                pltpu.VMEM((ext, DH), jnp.bfloat16),
                pltpu.VMEM((ext, DH), jnp.bfloat16),
                pltpu.VMEM((3, BT, BT), jnp.float32),
                pltpu.VMEM((BT, 1), jnp.float32),
                pltpu.VMEM((BT, 2 * DH), jnp.float32),
                pltpu.SemaphoreType.DMA((2, 3)),
            ],
        ),
        compiler_params=pltpu.CompilerParams(vmem_limit_bytes=12 * MIB),
        cost_estimate=pl.CostEstimate(
            flops=7 * 4 * tok_rows * BT * channels,
            transcendentals=7 * tok_rows * BT * heads,
            bytes_accessed=30 * MIB,
        ),
        name="band",
    )(meta, slopes, queries, key_rows, value_rows, before, after)


def gather_pieces(pieces, buffer_ref, sems, sources):
    if len(pieces) == 1:
        pieces = [pieces[0].at[s] for s in range(sources)]
    copies = [
        pltpu.make_async_copy(piece, buffer_ref.at[s], sems.at[s])
        for s, piece in enumerate(pieces)
    ]
    for copy in copies:
        copy.start()
    return copies


def place_of(slot, me, sources, split):
    source = lax.div(slot, CAP)
    if split:
        source = me - source
        source = jnp.where(source < 0, source + sources, source)
    return source, lax.rem(slot, CAP)


def far_kernel(
    meta_ref, slot_ref, block_ref, slopes_ref, query_ref, acc_ref, stat_ref, *refs, head, blk_dev,
    sources, group, split,
):
    if split:
        pieces = refs[:-6]
        weights_ref, out_ref, scale_ref, buffer_ref, bias_ref, sems = refs[-6:]
    else:
        pieces = refs[:-4]
        out_ref, buffer_ref, bias_ref, sems = refs[-4:]
    local = pl.program_id(0)
    slope = slopes_ref[head] * LOG2E

    @pl.when(local == 0)
    def _():
        copies = gather_pieces(pieces, buffer_ref, sems, sources)
        fill_bias(bias_ref, slope)
        for copy in copies:
            copy.wait()

    me = meta_ref[blk_dev]
    ones = jnp.ones((BT, DH), jnp.bfloat16)
    for part in range(group):
        i = local * group + part
        rows = pl.ds(part * BT, BT)
        block = me * blk_dev + i
        query = query_ref[rows, :]
        scores, values, shifts = [], [], []
        for f in range(FAR):
            apart = block - block_ref[f, i]
            sign = jnp.where(apart > 0, 0, jnp.where(apart < 0, 1, 2))
            shifts.append(slope * (jnp.abs(apart) * BT).astype(jnp.float32))
            source, rank = place_of(slot_ref[f, i], me, sources, split)
            key = buffer_ref[source, rank if split else rank * 2]
            scores.append(pair_scores(query, key, bias_ref[sign]))
            if split:
                values.append(ones)
            else:
                values.append(jnp.concatenate([buffer_ref[source, rank * 2 + 1], ones], axis=1))
        band = stat_ref[rows, :]
        top = jnp.maximum(
            band[:, 0:1],
            jnp.maximum(row_max(scores[0]) - shifts[0], row_max(scores[1]) - shifts[1]),
        )
        weights = [
            jnp.exp2(score - (top + shift)).astype(jnp.bfloat16)
            for score, shift in zip(scores, shifts)
        ]
        far = weighted(weights[0], values[0]) + weighted(weights[1], values[1])
        share = jnp.exp2(band - top)
        scale = 1.0 / (share + far[:, -DH:])
        acc = acc_ref[rows, :] * share
        if split:
            for f in range(FAR):
                weights_ref[rows, f * BT : (f + 1) * BT] = weights[f]
            out_ref[rows, :] = acc
            scale_ref[rows, :] = scale
        else:
            out_ref[rows, :] = ((acc + far[:, :DH]) * scale).astype(jnp.bfloat16)


def far_attention(meta, slots, far_blocks, slopes, queries, acc, stat, pieces, head, sources):
    tok_rows = queries.shape[0]
    blk_dev = tok_rows // BT
    split = len(pieces) > 1
    group = 2 if blk_dev % 2 == 0 else 1
    tile = pl.BlockSpec((group * BT, DH), lambda i, *_: (i, head))
    hbm = pl.BlockSpec(memory_space=pltpu.HBM)
    out_shape = [jax.ShapeDtypeStruct((tok_rows, DH), jnp.float32 if split else jnp.bfloat16)]
    out_specs = [pl.BlockSpec((group * BT, DH), lambda i, *_: (i, 0))]
    if split:
        out_shape = [
            pltpu.VMEM((tok_rows, FAR * BT), jnp.bfloat16),
            pltpu.VMEM((tok_rows, DH), jnp.float32),
            pltpu.VMEM((tok_rows, DH), jnp.float32),
        ]
        out_specs.append(out_specs[0])
        out_specs.insert(0, pl.BlockSpec((group * BT, FAR * BT), lambda i, *_: (i, 0)))
    return pl.pallas_call(
        functools.partial(
            far_kernel, head=head, blk_dev=blk_dev, sources=sources, group=group, split=split
        ),
        out_shape=out_shape,
        grid_spec=pltpu.PrefetchScalarGridSpec(
            num_scalar_prefetch=4,
            grid=(blk_dev // group,),
            in_specs=[tile, tile, tile] + [hbm] * len(pieces),
            out_specs=out_specs,
            scratch_shapes=[
                pltpu.VMEM((sources, CAP if split else CAP * 2, BT, DH), jnp.bfloat16),
                pltpu.VMEM((3, BT, BT), jnp.float32),
                pltpu.SemaphoreType.DMA((sources,)),
            ],
        ),
        compiler_params=pltpu.CompilerParams(vmem_limit_bytes=14 * MIB),
        cost_estimate=pl.CostEstimate(
            flops=2 * 4 * tok_rows * BT * DH,
            transcendentals=2 * tok_rows * BT,
            bytes_accessed=14 * MIB,
        ),
        name="far",
    )(meta, slots, far_blocks, slopes, queries, acc, stat, *pieces)


def value_kernel(me_ref, slot_ref, weights_ref, acc_ref, scale_ref, *refs, sources, blk_dev):
    pieces = refs[:-2]
    out_ref, buffer_ref = refs[-2:]
    for s, piece in enumerate(pieces):
        buffer_ref[s] = piece[...]
    for i in range(blk_dev):
        r = pl.ds(i * BT, BT)
        acc = acc_ref[r, :]
        for f in range(FAR):
            source, rank = place_of(slot_ref[f, i], me_ref[0], sources, True)
            acc = acc + weighted(weights_ref[r, f * BT : (f + 1) * BT], buffer_ref[source, rank])
        out_ref[r, :] = (acc * scale_ref[r, :]).astype(jnp.bfloat16)


def far_values(me, slots, weights, acc, scale, pieces, sources):
    tok_rows = acc.shape[0]
    blk_dev = tok_rows // BT
    smem = pl.BlockSpec(memory_space=pltpu.SMEM)
    vmem = pl.BlockSpec(memory_space=pltpu.VMEM)
    return pl.pallas_call(
        functools.partial(value_kernel, sources=sources, blk_dev=blk_dev),
        out_shape=pltpu.VMEM((tok_rows, DH), jnp.bfloat16),
        in_specs=[smem, smem] + [vmem] * (3 + len(pieces)),
        out_specs=vmem,
        scratch_shapes=[pltpu.VMEM((sources, CAP, BT, DH), jnp.bfloat16)],
        compiler_params=pltpu.CompilerParams(vmem_limit_bytes=4 * MIB),
        name="values",
    )(me, slots, weights, acc, scale, *pieces)


def place_kernel(*refs, heads):
    parts = refs[:heads]
    out_ref, sems = refs[heads:]
    peers = parts[0].shape[0]
    width = heads * DH
    copies = [
        pltpu.make_async_copy(
            part.at[g], out_ref.at[:, pl.ds(g * width + head * DH, DH)], sems.at[g, head]
        )
        for head, part in enumerate(parts)
        for g in range(peers)
    ]
    for copy in copies:
        copy.start()
    for copy in copies:
        copy.wait()


def place(parts):
    peers, rows, _ = parts[0].shape
    heads = len(parts)
    return pl.pallas_call(
        functools.partial(place_kernel, heads=heads),
        out_shape=jax.ShapeDtypeStruct((rows, peers * heads * DH), parts[0].dtype),
        in_specs=[pl.BlockSpec(memory_space=pltpu.VMEM)] * heads,
        out_specs=pl.BlockSpec(memory_space=pltpu.HBM),
        scratch_shapes=[pltpu.SemaphoreType.DMA((peers, heads))],
        name="place",
    )(*(pltpu.with_memory_space_constraint(part, pltpu.VMEM) for part in parts))


def body(queries, key_rows, value_rows, band_reach, far_list, slopes):
    myself = lax.axis_index("seq")
    sources = lax.axis_size("seq")
    tok_rows, channels = key_rows.shape
    blk_dev = tok_rows // BT
    heads = channels // DH
    up = [(i, i + 1) for i in range(sources - 1)]
    down = [(i + 1, i) for i in range(sources - 1)]

    keys_hbm, values_hbm = (
        pltpu.with_memory_space_constraint(x, pltpu.HBM) for x in (key_rows, value_rows)
    )
    table, slots = route(far_list, sources)
    last, first = halos(keys_hbm, values_hbm)
    columns = head_columns(keys_hbm, values_hbm, 0)
    asked = lax.all_to_all(table, "seq", split_axis=0, concat_axis=0, tiled=True)
    before = lax.ppermute(last, "seq", up)
    after = lax.ppermute(first, "seq", down)

    me = myself[None].astype(jnp.int32)
    incoming = []
    for head in range(heads):
        split = head == heads - 1
        source = columns if head == 0 else (keys_hbm, values_hbm)
        outgoing = pack(asked, me, *source, head, split)
        if split:
            pieces = []
            for which, kind in enumerate(("key", "value")):
                arrays = list(outgoing[which * sources : (which + 1) * sources])
                for shift in range(1, sources):
                    ring = [(i, (i + shift) % sources) for i in range(sources)]
                    arrays[shift] = lax.ppermute(arrays[shift], "seq", ring)
                space = pltpu.HBM if kind == "key" else pltpu.VMEM
                pieces.append([pltpu.with_memory_space_constraint(x, space) for x in arrays])
            incoming.append(pieces)
        else:
            incoming.append(
                [lax.all_to_all(outgoing[0], "seq", split_axis=0, concat_axis=0, tiled=True)]
            )

    meta = jnp.concatenate([band_reach, me])
    acc, stat = band_attention(
        meta, slopes, queries, key_rows, value_rows, before, after, blk_dev * sources
    )
    acc, stat, queries = (
        pltpu.with_memory_space_constraint(x, pltpu.HBM) for x in (acc, stat, queries)
    )
    parts = []
    for head in range(heads):
        split = head == heads - 1
        pieces = incoming[head][0] if split else incoming[head]
        attended = far_attention(
            meta, slots, far_list.T, slopes, queries, acc, stat, pieces, head, sources
        )
        if split:
            attended = far_values(me, slots, *attended, incoming[head][1], sources)
        else:
            attended = attended[0]
        parts.append(
            lax.all_to_all(
                attended.reshape(lax.axis_size("head"), -1, DH), "head",
                split_axis=0, concat_axis=0, tiled=True,
            )
        )
    return place(parts)


def solution(mesh):
    in_specs = (
        P("seq", "head"),
        P("seq", "head"),
        P("seq", "head"),
        P("seq"),
        P("seq", None),
        P("head"),
    )
    out_specs = P(("seq", "head"), None)

    return jax.shard_map(body, mesh=mesh, in_specs=in_specs, out_specs=out_specs, check_vma=False)
```

```python
import functools
import math

import jax
import jax.numpy as jnp
from jax import lax
from jax.experimental import pallas as pl
from jax.experimental.pallas import tpu as pltpu
from jax.sharding import PartitionSpec as P


BT = 256
BAND = 3
FAR = 2
CAP = 2
DH = 128
LOG2E = 1.4426950408889634
FAR_AWAY = 1e30
MIB = 1 << 20


def route_kernel(
    far_ref, keys_hbm, values_hbm, table_ref, slot_ref, last_ref, first_ref, count_ref, sems,
    *, sources, blk_dev,
):
    margin = BAND * BT
    copies = []
    for which, ref in enumerate((keys_hbm, values_hbm)):
        copies += [
            pltpu.make_async_copy(
                ref.at[pl.ds(blk_dev * BT - margin, margin)], last_ref.at[which], sems.at[which, 0]
            ),
            pltpu.make_async_copy(ref.at[pl.ds(0, margin)], first_ref.at[which], sems.at[which, 1]),
        ]
    for copy in copies:
        copy.start()
    for s in range(sources):
        count_ref[s] = 0
        for r in range(CAP):
            table_ref[s, r] = 0

    def step(i, carry):
        for f in range(FAR):
            block = far_ref[f, i]
            s = lax.div(block, blk_dev)
            r = jnp.minimum(count_ref[s], CAP - 1)
            count_ref[s] = r + 1
            table_ref[s, r] = block - s * blk_dev
            slot_ref[f, i] = s * CAP + r
        return carry

    lax.fori_loop(0, blk_dev, step, 0)
    for copy in copies:
        copy.wait()


def route(far_list, key_rows, value_rows, sources):
    blk_dev = far_list.shape[0]
    smem = pl.BlockSpec(memory_space=pltpu.SMEM)
    vmem = pl.BlockSpec(memory_space=pltpu.VMEM)
    hbm = pl.BlockSpec(memory_space=pltpu.HBM)
    halo = pltpu.VMEM((2, BAND * BT, key_rows.shape[1]), key_rows.dtype)
    return pl.pallas_call(
        functools.partial(route_kernel, sources=sources, blk_dev=blk_dev),
        out_shape=(
            jax.ShapeDtypeStruct((sources, CAP), jnp.int32),
            jax.ShapeDtypeStruct((FAR, blk_dev), jnp.int32),
            halo,
            halo,
        ),
        in_specs=[smem, hbm, hbm],
        out_specs=(smem, smem, vmem, vmem),
        scratch_shapes=[pltpu.SMEM((sources,), jnp.int32), pltpu.SemaphoreType.DMA((2, 2))],
        compiler_params=pltpu.CompilerParams(vmem_limit_bytes=4 * MIB),
        name="route",
    )(pltpu.with_memory_space_constraint(far_list.T, pltpu.HBM), key_rows, value_rows)


def stage_kernel(*refs, moves):
    sources, targets, sems = refs[:2], refs[2:-1], refs[-1]
    copies = [
        pltpu.make_async_copy(sources[which].at[rows, columns], target, sems.at[i])
        for i, (which, rows, columns, target) in enumerate(moves(targets))
    ]
    for copy in copies:
        copy.start()
    for copy in copies:
        copy.wait()


def stage(key_rows, value_rows, shapes, moves, count):
    vmem = pl.BlockSpec(memory_space=pltpu.VMEM)
    hbm = pl.BlockSpec(memory_space=pltpu.HBM)
    staged = pl.pallas_call(
        functools.partial(stage_kernel, moves=moves),
        out_shape=tuple(pltpu.VMEM(shape, key_rows.dtype) for shape in shapes),
        in_specs=[hbm, hbm],
        out_specs=(vmem,) * len(shapes),
        scratch_shapes=[pltpu.SemaphoreType.DMA((count,))],
        compiler_params=pltpu.CompilerParams(vmem_limit_bytes=4 * MIB),
    )(key_rows, value_rows)
    return [pltpu.with_memory_space_constraint(x, pltpu.VMEM) for x in staged]


def head_columns(key_rows, value_rows, head):
    tok_rows = key_rows.shape[0]

    def moves(targets):
        return [
            (which, pl.ds(0, tok_rows), pl.ds(head * DH, DH), target)
            for which, target in enumerate(targets)
        ]

    return stage(key_rows, value_rows, [(tok_rows, DH)] * 2, moves, 2)


def pack_kernel(asked_ref, me_ref, keys_ref, values_ref, *refs, shifts):
    out_refs, sems = refs[:-1], refs[-1]
    copies = []
    for which, ref in enumerate((keys_ref, values_ref)):
        for shift in range(shifts):
            target = me_ref[0] + shift
            target = jnp.where(target >= shifts, target - shifts, target)
            for r in range(CAP):
                rows = pl.ds(pl.multiple_of(asked_ref[target, r] * BT, BT), BT)
                slot = r * 2 + which
                if len(out_refs) == 1:
                    dst = out_refs[0].at[target, slot]
                else:
                    dst = out_refs[which * shifts + shift].at[r]
                copy = pltpu.make_async_copy(ref.at[rows, :], dst, sems.at[shift, slot])
                copy.start()
                copies.append(copy)
    for copy in copies:
        copy.wait()


def pack(asked, me, keys, values, head, split):
    shifts = asked.shape[0]
    tok_rows, channels = keys.shape
    hbm = pl.BlockSpec(memory_space=pltpu.HBM)
    if split:
        out_shape = (pltpu.HBM((CAP, BT, DH), keys.dtype),) * (2 * shifts)
    else:
        out_shape = (pltpu.HBM((shifts, CAP * 2, BT, DH), keys.dtype),)
    scratch = [pltpu.SemaphoreType.DMA((shifts, CAP * 2))]
    if channels == DH:
        smem = pl.BlockSpec(memory_space=pltpu.SMEM)
        vmem = pl.BlockSpec(memory_space=pltpu.VMEM)
        layout = dict(
            in_specs=[smem, smem, vmem, vmem],
            out_specs=(hbm,) * len(out_shape),
            scratch_shapes=scratch,
        )
    else:
        column = pl.BlockSpec((tok_rows, DH), lambda i, *_: (0, head))
        layout = dict(
            grid_spec=pltpu.PrefetchScalarGridSpec(
                num_scalar_prefetch=2,
                grid=(1,),
                in_specs=[column, column],
                out_specs=(hbm,) * len(out_shape),
                scratch_shapes=scratch,
            )
        )
    return pl.pallas_call(
        functools.partial(pack_kernel, shifts=shifts),
        out_shape=out_shape,
        compiler_params=pltpu.CompilerParams(vmem_limit_bytes=16 * MIB),
        name="pack",
        **layout,
    )(asked, me, keys, values)


def fill_bias(bias_ref, slope):
    rows = lax.broadcasted_iota(jnp.int32, (BT, BT), 0)
    columns = lax.broadcasted_iota(jnp.int32, (BT, BT), 1)
    gap = (rows - columns).astype(jnp.float32) * slope
    bias_ref[0] = gap
    bias_ref[1] = -gap
    bias_ref[2] = jnp.abs(gap)


def pair_scores(query, key, bias):
    product = lax.dot_general(
        query, key, (((1,), (1,)), ((), ())), preferred_element_type=jnp.float32
    )
    return product * (LOG2E / math.sqrt(DH)) - bias


def weighted(weights, value):
    return lax.dot_general(
        weights.astype(jnp.bfloat16), value, (((1,), (0,)), ((), ())),
        preferred_element_type=jnp.float32,
    )


def row_max(scores):
    return jnp.max(scores, axis=1, keepdims=True)


def band_kernel(
    meta_ref, slopes_ref, query_ref, keys_hbm, values_hbm, before_hbm, after_hbm,
    acc_ref, stat_ref,
    keys_ref, values_ref, bias_ref, max_ref, acc_ref2, sems, *, blk_dev, total_blocks,
):
    head = pl.program_id(0)
    local = pl.program_id(1)
    margin = BAND * BT
    tok_rows = blk_dev * BT
    slope = slopes_ref[head] * LOG2E

    @pl.when(local == 0)
    def _():
        column = pl.ds(pl.multiple_of(head * DH, DH), DH)
        copies = []
        for which, (ref, whole) in enumerate(((keys_ref, keys_hbm), (values_ref, values_hbm))):
            copies += [
                pltpu.make_async_copy(
                    before_hbm.at[which, :, column], ref.at[pl.ds(0, margin)], sems.at[which, 0]
                ),
                pltpu.make_async_copy(
                    whole.at[:, column], ref.at[pl.ds(margin, tok_rows)], sems.at[which, 1]
                ),
                pltpu.make_async_copy(
                    after_hbm.at[which, :, column],
                    ref.at[pl.ds(margin + tok_rows, margin)],
                    sems.at[which, 2],
                ),
            ]
        for copy in copies:
            copy.start()
        fill_bias(bias_ref, slope)
        for copy in copies:
            copy.wait()

    reach = meta_ref[local]
    block = meta_ref[blk_dev] * blk_dev + local
    query = query_ref[...]
    ones = jnp.ones((BT, DH), jnp.bfloat16)

    def rows_of(offset):
        return pl.ds(pl.multiple_of((local + BAND + offset) * BT, BT), BT)

    def value_of(offset):
        return jnp.concatenate([values_ref[rows_of(offset), :], ones], axis=1)

    scores = pair_scores(query, keys_ref[rows_of(0), :], bias_ref[2])
    top = row_max(scores)
    max_ref[...] = top
    acc_ref2[...] = weighted(jnp.exp2(scores - top), value_of(0))

    for distance in range(1, BAND + 1):

        @pl.when(reach >= distance)
        def _():
            low = slope * jnp.where(block >= distance, float(distance * BT), FAR_AWAY)
            high = slope * jnp.where(block + distance < total_blocks, float(distance * BT), FAR_AWAY)
            first = pair_scores(query, keys_ref[rows_of(-distance), :], bias_ref[0])
            second = pair_scores(query, keys_ref[rows_of(distance), :], bias_ref[1])
            old = max_ref[...]
            top = jnp.maximum(old, jnp.maximum(row_max(first) - low, row_max(second) - high))
            shrink = jnp.exp2(old - top)
            max_ref[...] = top
            acc_ref2[...] = (
                acc_ref2[...] * shrink
                + weighted(jnp.exp2(first - (top + low)), value_of(-distance))
                + weighted(jnp.exp2(second - (top + high)), value_of(distance))
            )

    total = acc_ref2[:, DH:]
    acc_ref[...] = acc_ref2[:, :DH] / total
    stat_ref[...] = max_ref[...] + jnp.log2(total)


def band_attention(meta, slopes, queries, key_rows, value_rows, before, after, total_blocks):
    tok_rows, channels = queries.shape
    blk_dev = tok_rows // BT
    heads = channels // DH
    any_spec = pl.BlockSpec(memory_space=pltpu.HBM)
    tile = pl.BlockSpec((BT, DH), lambda h, i, *_: (i, h))
    ext = tok_rows + 2 * BAND * BT
    return pl.pallas_call(
        functools.partial(band_kernel, blk_dev=blk_dev, total_blocks=total_blocks),
        out_shape=(
            jax.ShapeDtypeStruct((tok_rows, channels), jnp.float32),
            jax.ShapeDtypeStruct((tok_rows, channels), jnp.float32),
        ),
        grid_spec=pltpu.PrefetchScalarGridSpec(
            num_scalar_prefetch=2,
            grid=(heads, blk_dev),
            in_specs=[tile, any_spec, any_spec, any_spec, any_spec],
            out_specs=(tile, tile),
            scratch_shapes=[
                pltpu.VMEM((ext, DH), jnp.bfloat16),
                pltpu.VMEM((ext, DH), jnp.bfloat16),
                pltpu.VMEM((3, BT, BT), jnp.float32),
                pltpu.VMEM((BT, 1), jnp.float32),
                pltpu.VMEM((BT, 2 * DH), jnp.float32),
                pltpu.SemaphoreType.DMA((2, 3)),
            ],
        ),
        compiler_params=pltpu.CompilerParams(vmem_limit_bytes=12 * MIB),
        cost_estimate=pl.CostEstimate(
            flops=7 * 4 * tok_rows * BT * channels,
            transcendentals=7 * tok_rows * BT * heads,
            bytes_accessed=30 * MIB,
        ),
        name="band",
    )(meta, slopes, queries, key_rows, value_rows, before, after)


def gather_pieces(pieces, buffer_ref, sems, sources):
    if len(pieces) == 1:
        pieces = [pieces[0].at[s] for s in range(sources)]
    copies = [
        pltpu.make_async_copy(piece, buffer_ref.at[s], sems.at[s])
        for s, piece in enumerate(pieces)
    ]
    for copy in copies:
        copy.start()
    return copies


def place_of(slot, me, sources, split):
    source = lax.div(slot, CAP)
    if split:
        source = me - source
        source = jnp.where(source < 0, source + sources, source)
    return source, lax.rem(slot, CAP)


def far_kernel(
    meta_ref, slot_ref, block_ref, slopes_ref, query_ref, acc_ref, stat_ref, *refs, head, blk_dev,
    sources, group, split,
):
    if split:
        pieces = refs[:-6]
        weights_ref, out_ref, scale_ref, buffer_ref, bias_ref, sems = refs[-6:]
    else:
        pieces = refs[:-4]
        out_ref, buffer_ref, bias_ref, sems = refs[-4:]
    local = pl.program_id(0)
    slope = slopes_ref[head] * LOG2E

    @pl.when(local == 0)
    def _():
        copies = gather_pieces(pieces, buffer_ref, sems, sources)
        fill_bias(bias_ref, slope)
        for copy in copies:
            copy.wait()

    me = meta_ref[blk_dev]
    ones = jnp.ones((BT, DH), jnp.bfloat16)
    for part in range(group):
        i = local * group + part
        rows = pl.ds(part * BT, BT)
        block = me * blk_dev + i
        query = query_ref[rows, :]
        scores, values, shifts = [], [], []
        for f in range(FAR):
            apart = block - block_ref[f, i]
            sign = jnp.where(apart > 0, 0, jnp.where(apart < 0, 1, 2))
            shifts.append(slope * (jnp.abs(apart) * BT).astype(jnp.float32))
            source, rank = place_of(slot_ref[f, i], me, sources, split)
            key = buffer_ref[source, rank if split else rank * 2]
            scores.append(pair_scores(query, key, bias_ref[sign]))
            if split:
                values.append(ones)
            else:
                values.append(jnp.concatenate([buffer_ref[source, rank * 2 + 1], ones], axis=1))
        band = stat_ref[rows, :]
        top = jnp.maximum(
            band[:, 0:1],
            jnp.maximum(row_max(scores[0]) - shifts[0], row_max(scores[1]) - shifts[1]),
        )
        weights = [
            jnp.exp2(score - (top + shift)).astype(jnp.bfloat16)
            for score, shift in zip(scores, shifts)
        ]
        far = weighted(weights[0], values[0]) + weighted(weights[1], values[1])
        share = jnp.exp2(band - top)
        scale = 1.0 / (share + far[:, -DH:])
        acc = acc_ref[rows, :] * share
        if split:
            for f in range(FAR):
                weights_ref[rows, f * BT : (f + 1) * BT] = weights[f]
            out_ref[rows, :] = acc
            scale_ref[rows, :] = scale
        else:
            out_ref[rows, :] = ((acc + far[:, :DH]) * scale).astype(jnp.bfloat16)


def far_attention(meta, slots, far_blocks, slopes, queries, acc, stat, pieces, head, sources):
    tok_rows = queries.shape[0]
    blk_dev = tok_rows // BT
    split = len(pieces) > 1
    group = 2 if blk_dev % 2 == 0 else 1
    tile = pl.BlockSpec((group * BT, DH), lambda i, *_: (i, head))
    hbm = pl.BlockSpec(memory_space=pltpu.HBM)
    out_shape = [jax.ShapeDtypeStruct((tok_rows, DH), jnp.float32 if split else jnp.bfloat16)]
    out_specs = [pl.BlockSpec((group * BT, DH), lambda i, *_: (i, 0))]
    if split:
        out_shape = [
            pltpu.VMEM((tok_rows, FAR * BT), jnp.bfloat16),
            pltpu.VMEM((tok_rows, DH), jnp.float32),
            pltpu.VMEM((tok_rows, DH), jnp.float32),
        ]
        out_specs.append(out_specs[0])
        out_specs.insert(0, pl.BlockSpec((group * BT, FAR * BT), lambda i, *_: (i, 0)))
    return pl.pallas_call(
        functools.partial(
            far_kernel, head=head, blk_dev=blk_dev, sources=sources, group=group, split=split
        ),
        out_shape=out_shape,
        grid_spec=pltpu.PrefetchScalarGridSpec(
            num_scalar_prefetch=4,
            grid=(blk_dev // group,),
            in_specs=[tile, tile, tile] + [hbm] * len(pieces),
            out_specs=out_specs,
            scratch_shapes=[
                pltpu.VMEM((sources, CAP if split else CAP * 2, BT, DH), jnp.bfloat16),
                pltpu.VMEM((3, BT, BT), jnp.float32),
                pltpu.SemaphoreType.DMA((sources,)),
            ],
        ),
        compiler_params=pltpu.CompilerParams(vmem_limit_bytes=14 * MIB),
        cost_estimate=pl.CostEstimate(
            flops=2 * 4 * tok_rows * BT * DH,
            transcendentals=2 * tok_rows * BT,
            bytes_accessed=14 * MIB,
        ),
        name="far",
    )(meta, slots, far_blocks, slopes, queries, acc, stat, *pieces)


def value_kernel(me_ref, slot_ref, weights_ref, acc_ref, scale_ref, *refs, sources, blk_dev):
    pieces = refs[:-2]
    out_ref, buffer_ref = refs[-2:]
    for s, piece in enumerate(pieces):
        buffer_ref[s] = piece[...]
    for i in range(blk_dev):
        r = pl.ds(i * BT, BT)
        acc = acc_ref[r, :]
        for f in range(FAR):
            source, rank = place_of(slot_ref[f, i], me_ref[0], sources, True)
            acc = acc + weighted(weights_ref[r, f * BT : (f + 1) * BT], buffer_ref[source, rank])
        out_ref[r, :] = (acc * scale_ref[r, :]).astype(jnp.bfloat16)


def far_values(me, slots, weights, acc, scale, pieces, sources):
    tok_rows = acc.shape[0]
    blk_dev = tok_rows // BT
    smem = pl.BlockSpec(memory_space=pltpu.SMEM)
    vmem = pl.BlockSpec(memory_space=pltpu.VMEM)
    return pl.pallas_call(
        functools.partial(value_kernel, sources=sources, blk_dev=blk_dev),
        out_shape=pltpu.VMEM((tok_rows, DH), jnp.bfloat16),
        in_specs=[smem, smem] + [vmem] * (3 + len(pieces)),
        out_specs=vmem,
        scratch_shapes=[pltpu.VMEM((sources, CAP, BT, DH), jnp.bfloat16)],
        compiler_params=pltpu.CompilerParams(vmem_limit_bytes=4 * MIB),
        name="values",
    )(me, slots, weights, acc, scale, *pieces)


def place_kernel(*refs, heads):
    parts = refs[:heads]
    out_ref, sems = refs[heads:]
    peers = parts[0].shape[0]
    width = heads * DH
    copies = [
        pltpu.make_async_copy(
            part.at[g], out_ref.at[:, pl.ds(g * width + head * DH, DH)], sems.at[g, head]
        )
        for head, part in enumerate(parts)
        for g in range(peers)
    ]
    for copy in copies:
        copy.start()
    for copy in copies:
        copy.wait()


def place(parts):
    peers, rows, _ = parts[0].shape
    heads = len(parts)
    return pl.pallas_call(
        functools.partial(place_kernel, heads=heads),
        out_shape=jax.ShapeDtypeStruct((rows, peers * heads * DH), parts[0].dtype),
        in_specs=[pl.BlockSpec(memory_space=pltpu.VMEM)] * heads,
        out_specs=pl.BlockSpec(memory_space=pltpu.HBM),
        scratch_shapes=[pltpu.SemaphoreType.DMA((peers, heads))],
        name="place",
    )(*(pltpu.with_memory_space_constraint(part, pltpu.VMEM) for part in parts))


def body(queries, key_rows, value_rows, band_reach, far_list, slopes):
    myself = lax.axis_index("seq")
    sources = lax.axis_size("seq")
    tok_rows, channels = key_rows.shape
    blk_dev = tok_rows // BT
    heads = channels // DH
    up = [(i, i + 1) for i in range(sources - 1)]
    down = [(i + 1, i) for i in range(sources - 1)]

    keys_hbm, values_hbm = (
        pltpu.with_memory_space_constraint(x, pltpu.HBM) for x in (key_rows, value_rows)
    )
    table, slots, last, first = route(far_list, keys_hbm, values_hbm, sources)
    columns = head_columns(keys_hbm, values_hbm, 0)
    asked = lax.all_to_all(table, "seq", split_axis=0, concat_axis=0, tiled=True)
    before = lax.ppermute(last, "seq", up)
    after = lax.ppermute(first, "seq", down)

    me = myself[None].astype(jnp.int32)
    incoming = []
    for head in range(heads):
        split = head == heads - 1
        source = columns if head == 0 else (keys_hbm, values_hbm)
        outgoing = pack(asked, me, *source, head, split)
        if split:
            pieces = []
            for which, kind in enumerate(("key", "value")):
                arrays = list(outgoing[which * sources : (which + 1) * sources])
                for shift in range(1, sources):
                    ring = [(i, (i + shift) % sources) for i in range(sources)]
                    arrays[shift] = lax.ppermute(arrays[shift], "seq", ring)
                space = pltpu.HBM if kind == "key" else pltpu.VMEM
                pieces.append([pltpu.with_memory_space_constraint(x, space) for x in arrays])
            incoming.append(pieces)
        else:
            incoming.append(
                [lax.all_to_all(outgoing[0], "seq", split_axis=0, concat_axis=0, tiled=True)]
            )

    meta = jnp.concatenate([band_reach, me])
    acc, stat = band_attention(
        meta, slopes, queries, key_rows, value_rows, before, after, blk_dev * sources
    )
    acc, stat, queries = (
        pltpu.with_memory_space_constraint(x, pltpu.HBM) for x in (acc, stat, queries)
    )
    parts = []
    for head in range(heads):
        split = head == heads - 1
        pieces = incoming[head][0] if split else incoming[head]
        attended = far_attention(
            meta, slots, far_list.T, slopes, queries, acc, stat, pieces, head, sources
        )
        if split:
            attended = far_values(me, slots, *attended, incoming[head][1], sources)
        else:
            attended = attended[0]
        parts.append(
            lax.all_to_all(
                attended.reshape(lax.axis_size("head"), -1, DH), "head",
                split_axis=0, concat_axis=0, tiled=True,
            )
        )
    return place(parts)


def solution(mesh):
    in_specs = (
        P("seq", "head"),
        P("seq", "head"),
        P("seq", "head"),
        P("seq"),
        P("seq", None),
        P("head"),
    )
    out_specs = P(("seq", "head"), None)

    return jax.shard_map(body, mesh=mesh, in_specs=in_specs, out_specs=out_specs, check_vma=False)
```
